256 devices in a mesh: ctx: 64 (over y, z_hi, x, core), fsdp: 4 (over z_lo).
Axes of the slice: x: 4, y: 4, z: 8 (z_hi: 2, z_lo: 4; z = z_hi * 4 + z_lo), core: 2. Of those that a mesh axis runs over, the one named last changes fastest.
Arguments:
- tokens: bfloat16 [4, 16384, 2048], P('fsdp', 'ctx'), may hold values from -6 to 6
- qkv_weight: bfloat16 [3, 2048, 2048], P(None, None, 'fsdp'), may hold values from -0.125 to 0.125
- log_decay: float32 [4, 16, 16384], P('fsdp', None, 'ctx'), may hold values from -3 to 0
- norm_gain: float32 [2048], replicated, may hold values from 0.25 to 1.75
Outputs:
- normed: bfloat16 [4, 16384, 2048], P('fsdp', 'ctx')
The draws below stay inside these ranges and needn't reach their ends.
All inputs are finite; a program needn't handle non-finite values.
Results may differ from the reference program's by a relative error of at most 0.009.
Values may be sent and summed in bfloat16 or wider, within the bound.
No kernel may reach another device: no remote copies, remote signals or barrier semaphores. Data moves between devices by JAX's collectives and lax.ppermute only.
A program may use at most 192 MiB of HBM per device.

```python
import math
from functools import partial
import jax
import jax.numpy as jnp
from jax import lax

D = 2048
HEADS = 16
HEAD_DIM = 128
TOK_DEV = 256
TOKENS = 16384
SEQS = 4
INNER = 2048
N_CTX = 64


def draw_log_decay(key, part):
    keys_all = jax.random.split(jax.random.fold_in(key, 7), 5)
    slow_share = 0.5
    slow_heads = jax.random.uniform(keys_all[0], (SEQS, HEADS, 1), jnp.float32) < slow_share
    base_rate = jnp.where(slow_heads, 0.5 / TOKENS, 1.0 / 40.0)
    block_factor = jnp.exp(jax.random.uniform(keys_all[1], (SEQS, HEADS, TOKENS // TOK_DEV, 1), jnp.float32, math.log(0.5), math.log(2.0)))
    rough = jax.random.uniform(keys_all[2], (SEQS, HEADS, TOKENS // TOK_DEV, TOK_DEV), jnp.float32, 0.5, 1.5)
    constant_forget_factor = (rough * block_factor).reshape(SEQS, HEADS, TOKENS) * base_rate
    spots = jax.random.randint(keys_all[3], (SEQS, HEADS, 3, 1), 0, TOKENS)
    forget_strength_levels = jax.random.uniform(keys_all[4], (SEQS, HEADS, 3, 1), jnp.float32, math.log(0.5), math.log(0.8))
    forget_event_positions = jnp.arange(TOKENS, dtype=jnp.int32)[None, None, None, :] == spots
    forget_spike_groups = jnp.sum(jnp.where(forget_event_positions, forget_strength_levels, 0.0), axis=2)
    return (forget_spike_groups - constant_forget_factor).astype(jnp.float32)


def steps_of(stream_key, extent, pieces, low, largest):
    level, own = 1.0, jax.random.fold_in(stream_key, 6)
    for axis_at, blocks in pieces:
        heights = jnp.exp(jax.random.uniform(jax.random.fold_in(own, axis_at), (blocks,), jnp.float32, low / len(pieces), largest / len(pieces)))
        level = level * jnp.repeat(heights, extent[axis_at] // blocks).reshape([-1 if axis == axis_at else 1 for axis in range(len(extent))])
    return level


def noise(key, shape, scale, reach, shards=(), kind=jnp.bfloat16):
    loudness = steps_of(key, shape, shards, -0.22, 0.18) if shards else 1.0
    array = jax.random.normal(key, shape, jnp.float32) * scale * loudness
    return jnp.minimum(jnp.maximum(array, -reach), reach).astype(kind)


def setup_inputs(seed: int = 0) -> dict:
    streams_of = jax.random.split(jax.random.key(seed), 5)
    tokens = noise(streams_of[0], (SEQS, TOKENS, D), 1.0, 6.0, ((0, 4), (1, 64)))
    qkv_weight = noise(streams_of[1], (3, D, INNER), D ** -0.5, 0.125, ((2, 4),))
    log_decay = draw_log_decay(jax.random.fold_in(streams_of[4], 71), 0)
    norm_gain = jnp.clip(1.0 + 0.15 * jax.random.normal(streams_of[3], (INNER,), jnp.float32), 0.25, 1.75)
    return dict(tokens=tokens, qkv_weight=qkv_weight, log_decay=log_decay, norm_gain=norm_gain)


def block_step(state, packed, qkv_weight, norm_gain):
    block_in, rates = packed
    projected = [jnp.dot(block_in, qkv_weight[index], preferred_element_type=jnp.float32) for index in range(3)]
    queries = jax.nn.silu(projected[0]).astype(jnp.bfloat16).reshape(TOK_DEV, HEADS, HEAD_DIM)
    keys = jax.nn.silu(projected[1]).astype(jnp.bfloat16).reshape(TOK_DEV, HEADS, HEAD_DIM)
    values = projected[2].astype(jnp.bfloat16).reshape(TOK_DEV, HEADS, HEAD_DIM)
    cumulative = jnp.cumsum(rates, axis=1)
    log_gaps = cumulative[:, :, None] - cumulative[:, None, :]
    causal = jnp.arange(TOK_DEV)[:, None] >= jnp.arange(TOK_DEV)[None, :]
    factors = jnp.exp(jnp.where(causal[None], log_gaps, -jnp.inf))
    scores = jnp.einsum('thd,shd->hts', queries.astype(jnp.float32), keys.astype(jnp.float32))
    weights = (scores * factors).astype(jnp.bfloat16)
    inside = jnp.einsum('hts,shd->thd', weights.astype(jnp.float32), values.astype(jnp.float32))
    reduced_precision_memory = lax.optimization_barrier(state.astype(jnp.bfloat16))
    incoming = jnp.einsum('thd,hde->the', queries.astype(jnp.float32), reduced_precision_memory.astype(jnp.float32))
    incoming = incoming * jnp.exp(cumulative).T[:, :, None]
    attention_output = (inside + incoming).reshape(TOK_DEV, HEADS * HEAD_DIM)
    mean_sq = lax.optimization_barrier(jnp.mean(attention_output * attention_output, axis=-1, keepdims=True))
    normed = (attention_output * lax.rsqrt(mean_sq + 1e-05) * norm_gain).astype(jnp.bfloat16)
    tail = jnp.exp(cumulative[:, -1:] - cumulative)
    weighted_key_vectors = lax.optimization_barrier((keys.astype(jnp.float32) * tail.T[:, :, None]).astype(jnp.bfloat16))
    local = jnp.einsum('thd,the->hde', weighted_key_vectors.astype(jnp.float32), values.astype(jnp.float32))
    decay_total = jnp.exp(cumulative[:, -1])
    new_state = decay_total[:, None, None] * state + local
    return (new_state, normed)

def reference(tokens, qkv_weight, log_decay, norm_gain):

    def one_sequence(packed):
        seq_tokens, seq_rates = packed
        blocks = seq_tokens.reshape(N_CTX, TOK_DEV, D)
        rate_blocks = seq_rates.reshape(HEADS, N_CTX, TOK_DEV).transpose(1, 0, 2)
        initial = jnp.zeros((HEADS, HEAD_DIM, HEAD_DIM), jnp.float32)
        stepper = partial(block_step, qkv_weight=qkv_weight, norm_gain=norm_gain)
        last_state, outputs = lax.scan(stepper, initial, (blocks, rate_blocks))
        return outputs.reshape(TOKENS, HEADS * HEAD_DIM)
    return lax.map(one_sequence, (tokens, log_decay))
```

```python
import functools
import itertools

import jax
import jax.numpy as jnp
from jax import lax
from jax.experimental import pallas as pl
from jax.experimental.pallas import tpu as pltpu
from jax.sharding import PartitionSpec as P


F32 = jnp.float32
BF16 = jnp.bfloat16
BOTH = ("ctx", "fsdp")
VMEM = pl.BlockSpec(memory_space=pltpu.VMEM)
SMEM = pl.BlockSpec(memory_space=pltpu.SMEM)


def pairs(move):
    flat = lambda y, z, x, c: (((y * 2 + z // 4) * 4 + x) * 2 + c) * 4 + z % 4
    every = itertools.product(range(4), range(8), range(4), range(2))
    return [(flat(*at), flat(*move(*at))) for at in every]


def send(a, move):
    return lax.ppermute(a, BOTH, pairs(move))


def up(y, z, x, c):
    return y, (z + 1) % 8, x, c


def down(y, z, x, c):
    return y, (z - 1) % 8, x, c


def two(y, z, x, c):
    return y, (z + 2 - 4 * (z % 2)) % 8, x, c


def two_back(y, z, x, c):
    return y, (z - 2 + 4 * (z % 2)) % 8, x, c


def far(y, z, x, c):
    return y, (z + 4) % 8, x, c


def along_y(d):
    return lambda y, z, x, c: (y ^ d, z, x, c)


def along_row(d):
    def move(y, z, x, c):
        p = (x * 2 + c) ^ d
        return y, z, p // 2, p % 2

    return move


def silu(a):
    return a * jax.nn.sigmoid(a)


def dot(a, b, dims):
    return lax.dot_general(a, b, (dims, ((), ())), preferred_element_type=F32)


def state_kernel(tok, wk, wv, tail, k_out, v_out, local):
    t = tok[...]
    k = silu(jnp.dot(t, wk[0], preferred_element_type=F32)).astype(BF16)
    v = jnp.dot(t, wv[0], preferred_element_type=F32).astype(BF16)
    k_out[...] = k
    v_out[...] = v
    for h in range(2):
        cols = slice(128 * h, 128 * h + 128)
        scaled = (k[:, cols].astype(F32) * tail[0, :, h : h + 1]).astype(BF16)
        local[h] = dot(scaled, v[:, cols], ((0,), (0,))).astype(BF16)


def states(tok, weight, tail):
    n, d = tok.shape
    head2 = pl.BlockSpec((n, 256), lambda j: (0, j))
    return pl.pallas_call(
        state_kernel,
        grid=(2,),
        in_specs=[
            pl.BlockSpec((n, d), lambda j: (0, 0)),
            pl.BlockSpec((1, d, 256), lambda j: (1, 0, j)),
            pl.BlockSpec((1, d, 256), lambda j: (2, 0, j)),
            pl.BlockSpec((1, n, 2), lambda j: (j, 0, 0)),
        ],
        out_specs=[head2, head2, pl.BlockSpec((2, 128, 128), lambda j: (j, 0, 0))],
        out_shape=[
            jax.ShapeDtypeStruct((n, 512), BF16),
            jax.ShapeDtypeStruct((n, 512), BF16),
            jax.ShapeDtypeStruct((4, 128, 128), BF16),
        ],
        cost_estimate=pl.CostEstimate(flops=1 << 30, bytes_accessed=6 << 20, transcendentals=1 << 17),
        name="states",
    )(tok, weight, weight, tail)


def inside_kernel(tok, wq, k_ref, v_ref, col, row, out):
    q = silu(jnp.dot(tok[...], wq[0], preferred_element_type=F32)).astype(BF16)
    out[0] = q
    n = q.shape[0]
    causal = lax.broadcasted_iota(jnp.int32, (n, n), 0) >= lax.broadcasted_iota(jnp.int32, (n, n), 1)
    for h in range(2):
        cols = slice(128 * h, 128 * h + 128)
        scores = dot(q[:, cols], k_ref[:, cols], ((1,), (1,)))
        gaps = col[0, :, h : h + 1] - row[0, h : h + 1, :]
        weights = (scores * jnp.exp(jnp.where(causal, gaps, -jnp.inf))).astype(BF16)
        out[1, :, cols] = jnp.dot(weights, v_ref[:, cols], preferred_element_type=F32).astype(BF16)


def insides(tok, weight, k, v, col, row):
    n, d = tok.shape
    head2 = pl.BlockSpec((n, 256), lambda j: (0, j))
    return pl.pallas_call(
        inside_kernel,
        grid=(2,),
        in_specs=[
            pl.BlockSpec((n, d), lambda j: (0, 0)),
            pl.BlockSpec((1, d, 256), lambda j: (0, 0, j)),
            head2,
            head2,
            pl.BlockSpec((1, n, 2), lambda j: (j, 0, 0)),
            pl.BlockSpec((1, 2, n), lambda j: (j, 0, 0)),
        ],
        out_specs=pl.BlockSpec((2, n, 256), lambda j: (0, 0, j)),
        out_shape=jax.ShapeDtypeStruct((2, n, 512), BF16),
        cost_estimate=pl.CostEstimate(flops=1 << 30, bytes_accessed=5 << 20, transcendentals=1 << 19),
        name="insides",
    )(tok, weight, k, v, col, row)


def deal_kernel(at, s0, s1, s2, s3, *outs):
    p = at[0]
    for d in range(8):
        rows = pl.ds(pl.multiple_of(jnp.bitwise_xor(p, d) * 16, 16), 16)
        for i, s in enumerate((s0, s1, s2, s3)):
            outs[d][4 * i : 4 * i + 4] = s[:, rows, :]


PIECE = jax.ShapeDtypeStruct((16, 16, 128), BF16)


def deal(at, parts):
    return pl.pallas_call(
        deal_kernel,
        in_specs=[SMEM] + [VMEM] * 4,
        out_specs=[VMEM] * 8,
        out_shape=[PIECE] * 8,
        name="deal",
    )(at, *parts)


def total_kernel(at, decay, *refs):
    pieces, out, natural = refs[:8], refs[8], refs[9]
    p = at[0]
    for d in range(8):
        natural[jnp.bitwise_xor(p, d)] = pieces[d][...]
    for h in range(16):
        run = natural[0, h].astype(F32)
        for e in range(1, 8):
            run = run * decay[e, h] + natural[e, h].astype(F32)
        out[h] = run.astype(BF16)


def row_total(at, decay, pieces):
    return pl.pallas_call(
        total_kernel,
        in_specs=[SMEM, SMEM] + [VMEM] * 8,
        out_specs=VMEM,
        out_shape=PIECE,
        scratch_shapes=[pltpu.VMEM((8, 16, 16, 128), BF16)],
        name="row_total",
    )(at, decay, *pieces)


def carry_kernel(at, decay, row_decay, *refs):
    pieces, totals, outs, natural, rows = refs[:8], refs[8:16], refs[16:24], refs[24], refs[25]
    p, r = at[0], at[1]
    for d in range(8):
        natural[jnp.bitwise_xor(p, d)] = pieces[d][...]
        rows[jnp.bitwise_xor(r, d)] = totals[d][...]
    for h in range(16):
        run = jnp.zeros((16, 128), F32)
        for e in range(7):
            earlier = e < r
            run = run * row_decay[e, h] + jnp.where(earlier, rows[e, h].astype(F32), 0.0)
        for e in range(8):
            piece = natural[e, h].astype(F32)
            natural[e, h] = run.astype(BF16)
            run = run * decay[e, h] + piece
    for d in range(8):
        outs[d][...] = natural[jnp.bitwise_xor(p, d)]


def carry(at, decay, row_decay, pieces, totals):
    return pl.pallas_call(
        carry_kernel,
        in_specs=[SMEM] * 3 + [VMEM] * 16,
        out_specs=[VMEM] * 8,
        out_shape=[PIECE] * 8,
        scratch_shapes=[pltpu.VMEM((8, 16, 16, 128), BF16)] * 2,
        name="carry",
    )(at, decay, row_decay, *pieces, *totals)


def final_kernel(at, entry, gain, *refs):
    parts, pieces, out, memory, attended = refs[:4], refs[4:12], refs[12], refs[13], refs[14]
    p, f = at[0], at[2]
    for d in range(8):
        rows = pl.ds(pl.multiple_of(jnp.bitwise_xor(p, d) * 16, 16), 16)
        memory[:, rows, :] = pieces[d][...]
    squares = jnp.zeros((out.shape[0], 1), F32)
    for i, shift in enumerate((0, 1, 3, 2)):
        group = lax.rem(f + shift, 4)
        for h in range(4):
            cols = slice(128 * h, 128 * h + 128)
            incoming = jnp.dot(parts[i][0, :, cols], memory[4 * i + h], preferred_element_type=F32)
            value = parts[i][1, :, cols].astype(F32) + incoming * entry[:, 4 * i + h : 4 * i + h + 1]
            squares += jnp.sum(value * value, axis=-1, keepdims=True)
            attended[:, pl.ds(pl.multiple_of(group * 512 + 128 * h, 128), 128)] = value
    scale = lax.rsqrt(squares / out.shape[1] + 1e-05)
    out[...] = (attended[...] * scale * gain[...]).astype(BF16)


def final(at, entry, gain, parts, pieces):
    n, d = entry.shape[0], gain.shape[1]
    return pl.pallas_call(
        final_kernel,
        in_specs=[SMEM] + [VMEM] * 14,
        out_specs=VMEM,
        out_shape=jax.ShapeDtypeStruct((n, d), BF16),
        scratch_shapes=[pltpu.VMEM((16, 128, 128), BF16), pltpu.VMEM((n, d), F32)],
        name="final",
    )(at, entry, gain, *parts, *pieces)


def body(tokens, qkv_weight, log_decay, norm_gain):
    tok = tokens[0]
    rates = log_decay[0]
    n = tok.shape[0]
    i, f = lax.axis_index("ctx"), lax.axis_index("fsdp")
    p, r = i % 8, i // 8
    at = jnp.stack([p, r, f]).astype(jnp.int32)

    out_moves = (up, down, two)
    back_moves = (down, up, two_back)
    groups = rates.reshape(4, 4, n)
    mine = jnp.stack([lax.dynamic_index_in_dim(groups, (f + s) % 4, 0, False) for s in (0, 1, 3, 2)])
    slot_rates = jnp.stack([mine[0]] + [send(mine[s + 1], m) for s, m in enumerate(out_moves)])
    toks = [tok] + [send(tok, m) for m in out_moves]

    cum = jnp.cumsum(slot_rates, axis=-1)
    tail = jnp.exp(cum[:, :, -1:] - cum)
    by_pair = lambda a: a.reshape(4, 2, 2, n).transpose(0, 1, 3, 2)
    tail_col, cum_col, cum_row = by_pair(tail), by_pair(cum), cum.reshape(4, 2, 2, n)

    own_cum = jnp.cumsum(mine.reshape(16, n), axis=-1)
    entry = jnp.exp(own_cum).T
    block_log = own_cum[:, -1]
    spread = jnp.broadcast_to(jnp.pad(block_log, (0, 112))[None, None], (64, 8, 128))
    logs = lax.all_to_all(spread, "ctx", 0, 0, tiled=True)[:, 0, :16].reshape(8, 8, 16)
    decay = jnp.exp(lax.dynamic_index_in_dim(logs, r, 0, False))
    earlier = jnp.arange(8)[:, None] < r
    row_decay = jnp.exp(jnp.where(earlier, jnp.sum(logs, axis=1), 0.0))

    made = [states(toks[s], qkv_weight, tail_col[s]) for s in range(4)]
    owned = [made[0][2]] + [send(made[s + 1][2], m) for s, m in enumerate(back_moves)]
    parts = [
        insides(toks[s], qkv_weight, made[s][0], made[s][1], cum_col[s], cum_row[s]) for s in range(4)
    ]
    parts = [parts[0]] + [send(parts[s + 1], m) for s, m in enumerate(back_moves)]

    pieces = deal(at, owned)
    pieces = [pieces[0]] + [send(pieces[d], along_row(d)) for d in range(1, 8)]
    own_total = row_total(at, decay, pieces)
    far_total = send(own_total, far)
    totals = [own_total, far_total]
    for d in range(1, 4):
        totals += [send(own_total, along_y(d)), send(far_total, along_y(d))]
    carried = carry(at, decay, row_decay, pieces, totals)
    carried = [carried[0]] + [send(carried[d], along_row(d)) for d in range(1, 8)]
    return final(at, entry, norm_gain[None], parts, carried)[None]


def solution(mesh):
    placed = (P("fsdp", "ctx", None), P(None, None, "fsdp"), P("fsdp", None, "ctx"), P())
    return jax.shard_map(
        body, mesh=mesh, in_specs=placed, out_specs=P("fsdp", "ctx", None), check_vma=False
    )
```

```python
import itertools

import jax
import jax.numpy as jnp
from jax import lax
from jax.experimental import pallas as pl
from jax.experimental.pallas import tpu as pltpu
from jax.sharding import PartitionSpec as P


F32 = jnp.float32
BF16 = jnp.bfloat16
BOTH = ("ctx", "fsdp")
VMEM = pl.BlockSpec(memory_space=pltpu.VMEM)


def pairs(move):
    flat = lambda y, z, x, c: (((y * 2 + z // 4) * 4 + x) * 2 + c) * 4 + z % 4
    every = itertools.product(range(4), range(8), range(4), range(2))
    return [(flat(*at), flat(*move(*at))) for at in every]


def send(a, move):
    return lax.ppermute(a, BOTH, pairs(move))


def up(y, z, x, c):
    return y, (z + 1) % 8, x, c


def down(y, z, x, c):
    return y, (z - 1) % 8, x, c


def two(y, z, x, c):
    return y, (z + 2 - 4 * (z % 2)) % 8, x, c


def two_back(y, z, x, c):
    return y, (z - 2 + 4 * (z % 2)) % 8, x, c


def far(y, z, x, c):
    return y, (z + 4) % 8, x, c


def along_y(d):
    return lambda y, z, x, c: (y ^ d, z, x, c)


def along_row(d):
    def move(y, z, x, c):
        p = (x * 2 + c) ^ d
        return y, z, p // 2, p % 2

    return move


def silu(a):
    return a * jax.nn.sigmoid(a)


def dot(a, b, dims):
    return lax.dot_general(a, b, (dims, ((), ())), preferred_element_type=F32)


def call(kernel, outs, *args, flops=0, scratch=(), space=pltpu.VMEM, far=0):
    moved = sum(a.size * a.dtype.itemsize for a in args)
    near = len(args) - far
    held = [pltpu.with_memory_space_constraint(a, pltpu.VMEM) for a in args[:near]] + list(args[near:])
    return pl.pallas_call(
        kernel,
        in_specs=[VMEM] * near + [pl.BlockSpec(memory_space=pltpu.HBM)] * far,
        out_specs=[VMEM] * len(outs),
        out_shape=[space(shape, dtype) for shape, dtype in outs],
        scratch_shapes=[pltpu.VMEM(shape, dtype) for shape, dtype in scratch] + [pltpu.SemaphoreType.DMA(())] * far,
        cost_estimate=pl.CostEstimate(flops=flops, bytes_accessed=moved, transcendentals=0),
        compiler_params=pltpu.CompilerParams(vmem_limit_bytes=24 << 20),
    )(*held)


def place():
    i = lax.axis_index("ctx")
    return lax.rem(i, 8), lax.div(i, 8)


def running(a):
    lane = lax.broadcasted_iota(jnp.int32, a.shape, 1)
    for step in (1, 2, 4, 8, 16, 32, 64, 128):
        a = a + jnp.where(lane >= step, pltpu.roll(a, step, axis=1), 0.0)
    return a


SHIFTS = (0, 1, 3, 2)


def split(a):
    high = a.astype(BF16)
    rest = a - high.astype(F32)
    mid = rest.astype(BF16)
    return high, mid, (rest - mid.astype(F32)).astype(BF16)


def pack(column):
    lane = lax.broadcasted_iota(jnp.int32, (16, 128), 1)
    high, mid, low = (jnp.broadcast_to(a.astype(F32), (16, 128)) for a in split(column))
    return jnp.where(lane == 0, high, jnp.where(lane == 1, mid, jnp.where(lane == 2, low, 0.0))).astype(BF16)


def unpack(tile):
    a = tile.astype(F32)
    return a[:, 0:1] + a[:, 1:2] + a[:, 2:3]


def prepare(rates, tok, r0, r1, r2, r3, entry, total, held, sem):
    f = lax.axis_index("fsdp")
    copy = pltpu.make_async_copy(tok, held, sem)
    copy.start()
    cums = []
    for i, out in enumerate((r0, r1, r2, r3)):
        group = lax.rem(f + SHIFTS[i], 4)
        own = rates[0:4, :]
        for g in range(1, 4):
            own = jnp.where(group == g, rates[4 * g : 4 * g + 4, :], own)
        own = jnp.concatenate([own, jnp.zeros_like(own)], axis=0)
        out[...] = own
        cums.append(running(own)[:4])
    cum = jnp.concatenate(cums, axis=0)
    entry[...] = jnp.concatenate([jnp.exp(cum).T, jnp.zeros((256, 112), F32)], axis=1)
    total[...] = pack(cum[:, 255:256])
    copy.wait()


def load(w, held, sem):
    copy = pltpu.make_async_copy(w, held, sem)
    copy.start()
    copy.wait()


def states(tok, w, rates, *refs):
    k_out, v_out, local = refs[-3:]
    cum = running(rates[...])
    tail = jnp.exp(cum[:, 255:256] - cum).T
    for j in range(2):
        pair = slice(256 * j, 256 * j + 256)
        k = silu(jnp.dot(tok[...], w[1, :, pair], preferred_element_type=F32)).astype(BF16)
        v = jnp.dot(tok[...], w[2, :, pair], preferred_element_type=F32).astype(BF16)
        k_out[:, pair] = k
        v_out[:, pair] = v
        for h in range(2):
            cols = slice(128 * h, 128 * h + 128)
            head = 2 * j + h
            scaled = (k[:, cols].astype(F32) * tail[:, head : head + 1]).astype(BF16)
            local[head] = dot(scaled, v[:, cols], ((0,), (0,))).astype(BF16)


def insides(tok, w, rates, k_ref, v_ref, *refs):
    out = refs[-1]
    cum = running(rates[...])
    col = cum.T
    n = tok.shape[0]
    causal = lax.broadcasted_iota(jnp.int32, (n, n), 0) >= lax.broadcasted_iota(jnp.int32, (n, n), 1)
    for j in range(2):
        pair = slice(256 * j, 256 * j + 256)
        q = silu(jnp.dot(tok[...], w[0, :, pair], preferred_element_type=F32)).astype(BF16)
        out[0, :, pair] = q
        for h in range(2):
            head = 2 * j + h
            cols = slice(128 * head, 128 * head + 128)
            scores = dot(q[:, 128 * h : 128 * h + 128], k_ref[:, cols], ((1,), (1,)))
            gaps = col[:, head : head + 1] - cum[head : head + 1, :]
            weights = (scores * jnp.exp(jnp.where(causal, gaps, -jnp.inf))).astype(BF16)
            out[1, :, cols] = jnp.dot(weights, v_ref[:, cols], preferred_element_type=F32).astype(BF16)


def deal(s0, s1, s2, s3, total, *outs):
    p, _ = place()
    for d in range(8):
        rows = pl.ds(pl.multiple_of(jnp.bitwise_xor(p, d) * 16, 16), 16)
        for i, s in enumerate((s0, s1, s2, s3)):
            outs[d][4 * i : 4 * i + 4] = s[:, rows, :]
        outs[d][16] = total[...]


def row_total(*refs):
    pieces, out, natural, decay = refs[:8], refs[8], refs[9], refs[10]
    p, _ = place()
    for d in range(8):
        natural[jnp.bitwise_xor(p, d)] = pieces[d][...]
    logs = jnp.zeros((16, 1), F32)
    for e in range(8):
        own = unpack(natural[e, 16])
        logs += own
        decay[e] = jnp.broadcast_to(jnp.exp(own), (16, 128))
    for h in range(16):
        run = natural[0, h].astype(F32)
        for e in range(1, 8):
            run = run * decay[e, h : h + 1, :] + natural[e, h].astype(F32)
        out[h] = run.astype(BF16)
    out[16] = pack(logs)


def carry(*refs):
    pieces, totals, outs, natural, rows, decay, row_decay = refs[:8], refs[8:16], refs[16:24], *refs[24:]
    p, r = place()
    for d in range(8):
        natural[jnp.bitwise_xor(p, d)] = pieces[d][...]
        rows[jnp.bitwise_xor(r, d)] = totals[d][...]
    for e in range(8):
        decay[e] = jnp.broadcast_to(jnp.exp(unpack(natural[e, 16])), (16, 128))
        row_decay[e] = jnp.broadcast_to(jnp.exp(jnp.where(e < r, unpack(rows[e, 16]), 0.0)), (16, 128))
    for h in range(16):
        run = jnp.zeros((16, 128), F32)
        for e in range(7):
            run = run * row_decay[e, h : h + 1, :] + jnp.where(e < r, rows[e, h].astype(F32), 0.0)
        for e in range(8):
            piece = natural[e, h].astype(F32)
            natural[e, h] = run.astype(BF16)
            run = run * decay[e, h : h + 1, :] + piece
    for d in range(8):
        outs[d][...] = natural[jnp.bitwise_xor(p, d), 0:16]


def final(entry, gain, *refs):
    parts, pieces, out, memory, attended = refs[:4], refs[4:12], refs[12], refs[13], refs[14]
    p, _ = place()
    f = lax.axis_index("fsdp")
    for d in range(8):
        rows = pl.ds(pl.multiple_of(jnp.bitwise_xor(p, d) * 16, 16), 16)
        memory[:, rows, :] = pieces[d][...]
    squares = jnp.zeros((out.shape[0], 128), F32)
    for i, shift in enumerate(SHIFTS):
        group = lax.rem(f + shift, 4)
        for h in range(4):
            cols = slice(128 * h, 128 * h + 128)
            incoming = jnp.dot(parts[i][0, :, cols], memory[4 * i + h], preferred_element_type=F32)
            value = parts[i][1, :, cols].astype(F32) + incoming * entry[:, 4 * i + h : 4 * i + h + 1]
            squares += value * value
            attended[:, pl.ds(pl.multiple_of(group * 512 + 128 * h, 128), 128)] = value
    scale = lax.rsqrt(jnp.sum(squares, axis=-1, keepdims=True) / out.shape[1] + 1e-05)
    out[...] = (attended[...] * scale * gain[...]).astype(BF16)


def body(tokens, qkv_weight, log_decay, norm_gain):
    tok = tokens[0]
    n, d = tok.shape
    piece = ((17, 16, 128), BF16)
    slots = ((8, 17, 16, 128), BF16)
    factor = ((8, 16, 128), F32)

    back_moves = (down, up, two_back)
    *rates, entry, total, held = call(
        prepare,
        [((8, n), F32)] * 4 + [((n, 128), F32), ((16, 128), BF16), ((n, d), BF16)],
        log_decay[0],
        tok,
        far=1,
    )
    rates = [rates[0]] + [send(a, m) for a, m in zip(rates[1:], (up, down, two))]
    toks = [held, send(tok, up), send(tok, down)]
    toks.append(send(held, two))
    weight = call(load, [(qkv_weight.shape, BF16)], qkv_weight, far=1)[0]

    half = ((n, 512), BF16)
    made = []
    for t, a in zip(toks, rates):
        after = (made[0][2],) if made else ()
        made.append(
            call(states, [half, half, ((4, 128, 128), BF16)], t, weight, a, *after, flops=1 << 30)
        )
    owned = [made[0][2]] + [send(made[s + 1][2], m) for s, m in enumerate(back_moves)]
    pieces = call(deal, [piece] * 8, *owned, total)
    first = pieces[1]
    pieces = [pieces[0]] + [send(pieces[e], along_row(e)) for e in range(1, 8)]
    own_total = call(row_total, [piece], *pieces, scratch=[slots, factor])[0]

    after = ((), (made[3][2],), (first,), (own_total,))
    parts = []
    for i in range(4):
        out = ((2, n, 512), BF16)
        parts += call(insides, [out], toks[i], weight, rates[i], *made[i][:2], *after[i], flops=1 << 30)
    parts = [parts[0]] + [send(parts[i + 1], m) for i, m in enumerate(back_moves)]

    far_total = send(own_total, far)
    near = [send(own_total, along_y(e)) for e in range(1, 4)]
    totals = [own_total, far_total]
    for e in range(1, 4):
        totals += [near[e - 1], send(far_total, along_y(e))]
    carried = call(carry, [((16, 16, 128), BF16)] * 8, *pieces, *totals, scratch=[slots] * 2 + [factor] * 2)
    carried = [carried[0]] + [send(carried[e], along_row(e)) for e in range(1, 8)]
    out = call(
        final,
        [((n, d), BF16)],
        entry,
        norm_gain[None],
        *parts,
        *carried,
        scratch=[((16, 128, 128), BF16), ((n, d), F32)],
        space=jax.ShapeDtypeStruct,
    )[0]
    return out[None]


def solution(mesh):
    placed = (P("fsdp", "ctx", None), P(None, None, "fsdp"), P("fsdp", None, "ctx"), P())
    return jax.shard_map(body, mesh=mesh, in_specs=placed, out_specs=P("fsdp", "ctx", None), check_vma=False)
```

```python
import itertools

import jax
import jax.numpy as jnp
from jax import lax
from jax.experimental import pallas as pl
from jax.experimental.pallas import tpu as pltpu
from jax.sharding import PartitionSpec as P


F32 = jnp.float32
BF16 = jnp.bfloat16
BOTH = ("ctx", "fsdp")
VMEM = pl.BlockSpec(memory_space=pltpu.VMEM)


def pairs(move):
    flat = lambda y, z, x, c: (((y * 2 + z // 4) * 4 + x) * 2 + c) * 4 + z % 4
    every = itertools.product(range(4), range(8), range(4), range(2))
    return [(flat(*at), flat(*move(*at))) for at in every]


def send(a, move):
    return lax.ppermute(a, BOTH, pairs(move))


def up(y, z, x, c):
    return y, (z + 1) % 8, x, c


def down(y, z, x, c):
    return y, (z - 1) % 8, x, c


def two(y, z, x, c):
    return y, (z + 2 - 4 * (z % 2)) % 8, x, c


def two_back(y, z, x, c):
    return y, (z - 2 + 4 * (z % 2)) % 8, x, c


def far(y, z, x, c):
    return y, (z + 4) % 8, x, c


def along_y(d):
    return lambda y, z, x, c: (y ^ d, z, x, c)


def along_row(d):
    def move(y, z, x, c):
        p = (x * 2 + c) ^ d
        return y, z, p // 2, p % 2

    return move


def silu(a):
    return a * jax.nn.sigmoid(a)


def dot(a, b, dims):
    return lax.dot_general(a, b, (dims, ((), ())), preferred_element_type=F32)


def call(kernel, outs, *args, flops=0, scratch=(), space=pltpu.VMEM, far=0):
    moved = sum(a.size * a.dtype.itemsize for a in args)
    near = len(args) - far
    held = [pltpu.with_memory_space_constraint(a, pltpu.VMEM) for a in args[:near]] + [
        pltpu.with_memory_space_constraint(a, pltpu.HBM) for a in args[near:]
    ]
    return pl.pallas_call(
        kernel,
        in_specs=[VMEM] * near + [pl.BlockSpec(memory_space=pltpu.HBM)] * far,
        out_specs=[VMEM] * len(outs),
        out_shape=[space(shape, dtype) for shape, dtype in outs],
        scratch_shapes=[pltpu.VMEM(shape, dtype) for shape, dtype in scratch] + [pltpu.SemaphoreType.DMA(())] * far,
        cost_estimate=pl.CostEstimate(flops=flops, bytes_accessed=moved, transcendentals=0),
        compiler_params=pltpu.CompilerParams(vmem_limit_bytes=24 << 20),
    )(*held)


def place():
    i = lax.axis_index("ctx")
    return lax.rem(i, 8), lax.div(i, 8)


def running(a):
    lane = lax.broadcasted_iota(jnp.int32, a.shape, 1)
    for step in (1, 2, 4, 8, 16, 32, 64, 128):
        a = a + jnp.where(lane >= step, pltpu.roll(a, step, axis=1), 0.0)
    return a


SHIFTS = (0, 1, 3, 2)


def split(a):
    high = a.astype(BF16)
    rest = a - high.astype(F32)
    mid = rest.astype(BF16)
    return high, mid, (rest - mid.astype(F32)).astype(BF16)


def pack(column):
    lane = lax.broadcasted_iota(jnp.int32, (16, 128), 1)
    high, mid, low = (jnp.broadcast_to(a.astype(F32), (16, 128)) for a in split(column))
    return jnp.where(lane == 0, high, jnp.where(lane == 1, mid, jnp.where(lane == 2, low, 0.0))).astype(BF16)


def unpack(tile):
    a = tile.astype(F32)
    return a[:, 0:1] + a[:, 1:2] + a[:, 2:3]


def prepare(rates, tok, r0, r1, r2, r3, entry, total, held, sem):
    f = lax.axis_index("fsdp")
    copy = pltpu.make_async_copy(tok, held, sem)
    copy.start()
    cums = []
    for i, out in enumerate((r0, r1, r2, r3)):
        group = lax.rem(f + SHIFTS[i], 4)
        own = rates[0:4, :]
        for g in range(1, 4):
            own = jnp.where(group == g, rates[4 * g : 4 * g + 4, :], own)
        own = jnp.concatenate([own, jnp.zeros_like(own)], axis=0)
        out[...] = own
        cums.append(running(own)[:4])
    cum = jnp.concatenate(cums, axis=0)
    entry[...] = jnp.concatenate([jnp.exp(cum).T, jnp.zeros((256, 112), F32)], axis=1)
    total[...] = pack(cum[:, 255:256])
    copy.wait()


def load(w, held, sem):
    copy = pltpu.make_async_copy(w, held, sem)
    copy.start()
    copy.wait()


def states(tok, w, rates, *refs):
    k_out, v_out, local = refs[-3:]
    cum = running(rates[...])
    tail = jnp.exp(cum[:, 255:256] - cum).T
    for j in range(2):
        pair = slice(256 * j, 256 * j + 256)
        k = silu(jnp.dot(tok[...], w[1, :, pair], preferred_element_type=F32)).astype(BF16)
        v = jnp.dot(tok[...], w[2, :, pair], preferred_element_type=F32).astype(BF16)
        k_out[:, pair] = k
        v_out[:, pair] = v
        for h in range(2):
            cols = slice(128 * h, 128 * h + 128)
            head = 2 * j + h
            scaled = (k[:, cols].astype(F32) * tail[:, head : head + 1]).astype(BF16)
            local[head] = dot(scaled, v[:, cols], ((0,), (0,))).astype(BF16)


def insides(tok, w, rates, k_ref, v_ref, *refs):
    out = refs[-1]
    cum = running(rates[...])
    col = cum.T
    n = tok.shape[0]
    causal = lax.broadcasted_iota(jnp.int32, (n, n), 0) >= lax.broadcasted_iota(jnp.int32, (n, n), 1)
    for j in range(2):
        pair = slice(256 * j, 256 * j + 256)
        q = silu(jnp.dot(tok[...], w[0, :, pair], preferred_element_type=F32)).astype(BF16)
        out[0, :, pair] = q
        for h in range(2):
            head = 2 * j + h
            cols = slice(128 * head, 128 * head + 128)
            scores = dot(q[:, 128 * h : 128 * h + 128], k_ref[:, cols], ((1,), (1,)))
            gaps = col[:, head : head + 1] - cum[head : head + 1, :]
            weights = (scores * jnp.exp(jnp.where(causal, gaps, -jnp.inf))).astype(BF16)
            out[1, :, cols] = jnp.dot(weights, v_ref[:, cols], preferred_element_type=F32).astype(BF16)


def deal(s0, s1, s2, s3, total, *outs):
    p, _ = place()
    for d in range(8):
        rows = pl.ds(pl.multiple_of(jnp.bitwise_xor(p, d) * 16, 16), 16)
        for i, s in enumerate((s0, s1, s2, s3)):
            outs[d][4 * i : 4 * i + 4] = s[:, rows, :]
        outs[d][16] = total[...]


def row_total(*refs):
    pieces, out, natural, decay = refs[:8], refs[8], refs[9], refs[10]
    p, _ = place()
    for d in range(8):
        natural[jnp.bitwise_xor(p, d)] = pieces[d][...]
    logs = jnp.zeros((16, 1), F32)
    for e in range(8):
        own = unpack(natural[e, 16])
        logs += own
        decay[e] = jnp.broadcast_to(jnp.exp(own), (16, 128))
    for h in range(16):
        run = natural[0, h].astype(F32)
        for e in range(1, 8):
            run = run * decay[e, h : h + 1, :] + natural[e, h].astype(F32)
        out[h] = run.astype(BF16)
    out[16] = pack(logs)


def carry(*refs):
    pieces, totals, outs, natural, rows, decay, row_decay = refs[:8], refs[8:16], refs[16:24], *refs[24:]
    p, r = place()
    for d in range(8):
        natural[jnp.bitwise_xor(p, d)] = pieces[d][...]
        rows[jnp.bitwise_xor(r, d)] = totals[d][...]
    for e in range(8):
        decay[e] = jnp.broadcast_to(jnp.exp(unpack(natural[e, 16])), (16, 128))
        row_decay[e] = jnp.broadcast_to(jnp.exp(jnp.where(e < r, unpack(rows[e, 16]), 0.0)), (16, 128))
    for h in range(16):
        run = jnp.zeros((16, 128), F32)
        for e in range(7):
            run = run * row_decay[e, h : h + 1, :] + jnp.where(e < r, rows[e, h].astype(F32), 0.0)
        for e in range(8):
            piece = natural[e, h].astype(F32)
            natural[e, h] = run.astype(BF16)
            run = run * decay[e, h : h + 1, :] + piece
    for d in range(8):
        outs[d][...] = natural[jnp.bitwise_xor(p, d), 0:16]


def final(entry, gain, *refs):
    parts, pieces, out, memory, attended = refs[:4], refs[4:12], refs[12], refs[13], refs[14]
    p, _ = place()
    f = lax.axis_index("fsdp")
    for d in range(8):
        rows = pl.ds(pl.multiple_of(jnp.bitwise_xor(p, d) * 16, 16), 16)
        memory[:, rows, :] = pieces[d][...]
    squares = jnp.zeros((out.shape[0], 128), F32)
    for i, shift in enumerate(SHIFTS):
        group = lax.rem(f + shift, 4)
        for h in range(4):
            cols = slice(128 * h, 128 * h + 128)
            incoming = jnp.dot(parts[i][0, :, cols], memory[4 * i + h], preferred_element_type=F32)
            value = parts[i][1, :, cols].astype(F32) + incoming * entry[:, 4 * i + h : 4 * i + h + 1]
            squares += value * value
            attended[:, pl.ds(pl.multiple_of(group * 512 + 128 * h, 128), 128)] = value
    scale = lax.rsqrt(jnp.sum(squares, axis=-1, keepdims=True) / out.shape[1] + 1e-05)
    out[...] = (attended[...] * scale * gain[...]).astype(BF16)


def body(tokens, qkv_weight, log_decay, norm_gain):
    tok = tokens[0]
    n, d = tok.shape
    piece = ((17, 16, 128), BF16)
    slots = ((8, 17, 16, 128), BF16)
    factor = ((8, 16, 128), F32)

    back_moves = (down, up, two_back)
    *rates, entry, total, held = call(
        prepare,
        [((8, n), F32)] * 4 + [((n, 128), F32), ((16, 128), BF16), ((n, d), BF16)],
        log_decay[0],
        tok,
        far=1,
    )
    rates = [rates[0]] + [send(a, m) for a, m in zip(rates[1:], (up, down, two))]
    toks = [held, send(tok, up), send(tok, down)]
    toks.append(send(tok, two))
    weight = call(load, [(qkv_weight.shape, BF16)], qkv_weight, far=1)[0]

    half = ((n, 512), BF16)
    made = []
    for t, a in zip(toks, rates):
        after = (made[0][2],) if made else ()
        made.append(
            call(states, [half, half, ((4, 128, 128), BF16)], t, weight, a, *after, flops=1 << 30)
        )
    owned = [made[0][2]]
    for s, m in enumerate(back_moves):
        owned.append(send(made[s + 1][2], m))
    pieces = call(deal, [piece] * 8, *owned, total)
    pieces = [pieces[0]] + [send(pieces[e], along_row(e)) for e in range(1, 8)]
    own_total = call(row_total, [piece], *pieces, scratch=[slots, factor])[0]

    after = ((), (made[3][2],), (made[3][2],), (own_total,))
    parts = []
    for i in range(4):
        out = ((2, n, 512), BF16)
        parts += call(insides, [out], toks[i], weight, rates[i], *made[i][:2], *after[i], flops=1 << 30)
    for i, m in enumerate(back_moves):
        parts[i + 1] = send(parts[i + 1], m)

    far_total = send(own_total, far)
    near = [send(own_total, along_y(e)) for e in range(1, 4)]
    totals = [own_total, far_total]
    for e in range(1, 4):
        totals += [near[e - 1], send(far_total, along_y(e))]
    carried = call(carry, [((16, 16, 128), BF16)] * 8, *pieces, *totals, scratch=[slots] * 2 + [factor] * 2)
    carried = [carried[0]] + [send(carried[e], along_row(e)) for e in range(1, 8)]
    out = call(
        final,
        [((n, d), BF16)],
        entry,
        norm_gain[None],
        *parts,
        *carried,
        scratch=[((16, 128, 128), BF16), ((n, d), F32)],
        space=jax.ShapeDtypeStruct,
    )[0]
    return out[None]


def solution(mesh):
    placed = (P("fsdp", "ctx", None), P(None, None, "fsdp"), P("fsdp", None, "ctx"), P())
    return jax.shard_map(body, mesh=mesh, in_specs=placed, out_specs=P("fsdp", "ctx", None), check_vma=False)
```

```python
import itertools

import jax
import jax.numpy as jnp
from jax import lax
from jax.experimental import pallas as pl
from jax.experimental.pallas import tpu as pltpu
from jax.sharding import PartitionSpec as P


F32 = jnp.float32
BF16 = jnp.bfloat16
BOTH = ("ctx", "fsdp")
VMEM = pl.BlockSpec(memory_space=pltpu.VMEM)


def pairs(move):
    flat = lambda y, z, x, c: (((y * 2 + z // 4) * 4 + x) * 2 + c) * 4 + z % 4
    every = itertools.product(range(4), range(8), range(4), range(2))
    return [(flat(*at), flat(*move(*at))) for at in every]


def send(a, move):
    return lax.ppermute(a, BOTH, pairs(move))


def up(y, z, x, c):
    return y, (z + 1) % 8, x, c


def down(y, z, x, c):
    return y, (z - 1) % 8, x, c


def two(y, z, x, c):
    return y, (z + 2 - 4 * (z % 2)) % 8, x, c


def two_back(y, z, x, c):
    return y, (z - 2 + 4 * (z % 2)) % 8, x, c


def other(y, z, x, c):
    return y, z, x, 1 - c


def crossed(move):
    return lambda *at: other(*move(*at))


def along_x(d):
    return lambda y, z, x, c: (y, z, x ^ d, c)


def far(y, z, x, c):
    return y, (z + 4) % 8, x, c


def along_y(d):
    return lambda y, z, x, c: (y ^ d, z, x, c)


def exchange(parts, order, move):
    got = {d: send(parts[d], move(d)) for d in order}
    return [parts[0]] + [got[d] for d in range(1, len(parts))]


def along_row(d):
    def move(y, z, x, c):
        p = (x * 2 + c) ^ d
        return y, z, p // 2, p % 2

    return move


def silu(a):
    return a * jax.nn.sigmoid(a)


def dot(a, b, dims):
    return lax.dot_general(a, b, (dims, ((), ())), preferred_element_type=F32)


def call(kernel, outs, *args, flops=0, scratch=(), space=pltpu.VMEM, far=0):
    moved = sum(a.size * a.dtype.itemsize for a in args)
    near = len(args) - far
    held = [pltpu.with_memory_space_constraint(a, pltpu.VMEM) for a in args[:near]] + [
        pltpu.with_memory_space_constraint(a, pltpu.HBM) for a in args[near:]
    ]
    return pl.pallas_call(
        kernel,
        in_specs=[VMEM] * near + [pl.BlockSpec(memory_space=pltpu.HBM)] * far,
        out_specs=[VMEM] * len(outs),
        out_shape=[space(shape, dtype) for shape, dtype in outs],
        scratch_shapes=[pltpu.VMEM(shape, dtype) for shape, dtype in scratch] + [pltpu.SemaphoreType.DMA(())] * far,
        cost_estimate=pl.CostEstimate(flops=flops, bytes_accessed=moved, transcendentals=0),
        compiler_params=pltpu.CompilerParams(vmem_limit_bytes=24 << 20),
    )(*held)


def place():
    i = lax.axis_index("ctx")
    return lax.rem(i, 8), lax.div(i, 8)


def running(a):
    lane = lax.broadcasted_iota(jnp.int32, a.shape, 1)
    for step in (1, 2, 4, 8, 16, 32, 64, 128):
        a = a + jnp.where(lane >= step, pltpu.roll(a, step, axis=1), 0.0)
    return a


SHIFTS = (0, 1, 3, 2)


def split(a):
    high = a.astype(BF16)
    rest = a - high.astype(F32)
    mid = rest.astype(BF16)
    return high, mid, (rest - mid.astype(F32)).astype(BF16)


def pack(column):
    lane = lax.broadcasted_iota(jnp.int32, (16, 128), 1)
    high, mid, low = (jnp.broadcast_to(a.astype(F32), (16, 128)) for a in split(column))
    return jnp.where(lane == 0, high, jnp.where(lane == 1, mid, jnp.where(lane == 2, low, 0.0))).astype(BF16)


def unpack(tile):
    a = tile.astype(F32)
    return a[:, 0:1] + a[:, 1:2] + a[:, 2:3]


def prepare(rates, tok, r0, r1, r2, r3, entry, total, held, sem):
    f = lax.axis_index("fsdp")
    copy = pltpu.make_async_copy(tok, held, sem)
    copy.start()
    cums = []
    for i, out in enumerate((r0, r1, r2, r3)):
        group = lax.rem(f + SHIFTS[i], 4)
        own = rates[0:4, :]
        for g in range(1, 4):
            own = jnp.where(group == g, rates[4 * g : 4 * g + 4, :], own)
        own = jnp.concatenate([own, jnp.zeros_like(own)], axis=0)
        out[...] = own
        cums.append(running(own)[:4])
    cum = jnp.concatenate(cums, axis=0)
    entry[...] = jnp.concatenate([jnp.exp(cum).T, jnp.zeros((256, 112), F32)], axis=1)
    total[...] = pack(cum[:, 255:256])
    copy.wait()


def load(w, held, sem):
    copy = pltpu.make_async_copy(w, held, sem)
    copy.start()
    copy.wait()


def states(tok, w, rates, *refs):
    k_out, v_out, same, cross, local = refs[-5:]
    cum = running(rates[...])
    tail = jnp.exp(cum[:, 255:256] - cum).T
    for j in range(2):
        pair = slice(256 * j, 256 * j + 256)
        k = silu(jnp.dot(tok[...], w[1, :, pair], preferred_element_type=F32)).astype(BF16)
        v = jnp.dot(tok[...], w[2, :, pair], preferred_element_type=F32).astype(BF16)
        k_out[:, pair] = k
        v_out[:, pair] = v
        for h in range(2):
            cols = slice(128 * h, 128 * h + 128)
            head = 2 * j + h
            scaled = (k[:, cols].astype(F32) * tail[:, head : head + 1]).astype(BF16)
            local[head] = dot(scaled, v[:, cols], ((0,), (0,))).astype(BF16)
    core = lax.rem(place()[0], 2)
    same[...] = local[:, pl.ds(pl.multiple_of(core * 64, 64), 64), :]
    cross[...] = local[:, pl.ds(pl.multiple_of((1 - core) * 64, 64), 64), :]


def insides(tok, w, rates, k_ref, v_ref, *refs):
    out = refs[-1]
    cum = running(rates[...])
    col = cum.T
    n = tok.shape[0]
    causal = lax.broadcasted_iota(jnp.int32, (n, n), 0) >= lax.broadcasted_iota(jnp.int32, (n, n), 1)
    for j in range(2):
        pair = slice(256 * j, 256 * j + 256)
        q = silu(jnp.dot(tok[...], w[0, :, pair], preferred_element_type=F32)).astype(BF16)
        out[0, :, pair] = q
        for h in range(2):
            head = 2 * j + h
            cols = slice(128 * head, 128 * head + 128)
            scores = dot(q[:, 128 * h : 128 * h + 128], k_ref[:, cols], ((1,), (1,)))
            gaps = col[:, head : head + 1] - cum[head : head + 1, :]
            weights = (scores * jnp.exp(jnp.where(causal, gaps, -jnp.inf))).astype(BF16)
            out[1, :, cols] = jnp.dot(weights, v_ref[:, cols], preferred_element_type=F32).astype(BF16)


def deal(*refs):
    own, partner, (total, partner_total), outs = refs[:4], refs[4:8], refs[8:10], refs[10:]
    p, _ = place()
    x, core = lax.div(p, 2), lax.rem(p, 2)
    for d in range(4):
        rows = pl.ds(pl.multiple_of(jnp.bitwise_xor(x, d) * 16, 16), 16)
        for block, parts, log in ((core, own, total), (1 - core, partner, partner_total)):
            for i, s in enumerate(parts):
                outs[d][block, 4 * i : 4 * i + 4] = s[:, rows, :]
            outs[d][block, 16] = log[...]


def arrange(natural, pieces):
    x = lax.div(place()[0], 2)
    for d in range(4):
        at = jnp.bitwise_xor(x, d) * 2
        for core in range(2):
            natural[at + core] = pieces[d][core]


def row_total(*refs):
    pieces, out, natural, decay = refs[:4], refs[4], refs[5], refs[6]
    arrange(natural, pieces)
    logs = jnp.zeros((16, 1), F32)
    for e in range(8):
        own = unpack(natural[e, 16])
        logs += own
        decay[e] = jnp.broadcast_to(jnp.exp(own), (16, 128))
    for h in range(16):
        run = natural[0, h].astype(F32)
        for e in range(1, 8):
            run = run * decay[e, h : h + 1, :] + natural[e, h].astype(F32)
        out[h] = run.astype(BF16)
    out[16] = pack(logs)


def mark(total, out):
    out[...] = total[16]


def carry(_, *refs):
    pieces, totals, outs, natural, rows, decay, row_decay = refs[:4], refs[4:12], refs[12:20], *refs[20:]
    p, r = place()
    arrange(natural, pieces)
    for d in range(8):
        rows[jnp.bitwise_xor(r, d)] = totals[d][...]
    for e in range(8):
        decay[e] = jnp.broadcast_to(jnp.exp(unpack(natural[e, 16])), (16, 128))
        row_decay[e] = jnp.broadcast_to(jnp.exp(jnp.where(e < r, unpack(rows[e, 16]), 0.0)), (16, 128))
    for h in range(16):
        run = jnp.zeros((16, 128), F32)
        for e in range(7):
            run = run * row_decay[e, h : h + 1, :] + jnp.where(e < r, rows[e, h].astype(F32), 0.0)
        for e in range(8):
            piece = natural[e, h].astype(F32)
            natural[e, h] = run.astype(BF16)
            run = run * decay[e, h : h + 1, :] + piece
    for d in range(8):
        outs[d][...] = natural[jnp.bitwise_xor(p, d), 0:16]


def final(entry, gain, *refs):
    parts, pieces, out, memory, attended = refs[:4], refs[4:12], refs[12], refs[13], refs[14]
    p, _ = place()
    f = lax.axis_index("fsdp")
    for d in range(8):
        sender = jnp.bitwise_xor(p, d)
        piece = lax.rem(sender, 2) * 4 + lax.div(sender, 2)
        memory[:, pl.ds(pl.multiple_of(piece * 16, 16), 16), :] = pieces[d][...]
    squares = jnp.zeros((out.shape[0], 128), F32)
    for i, shift in enumerate(SHIFTS):
        group = lax.rem(f + shift, 4)
        for h in range(4):
            cols = slice(128 * h, 128 * h + 128)
            incoming = jnp.dot(parts[i][0, :, cols], memory[4 * i + h], preferred_element_type=F32)
            value = parts[i][1, :, cols].astype(F32) + incoming * entry[:, 4 * i + h : 4 * i + h + 1]
            squares += value * value
            attended[:, pl.ds(pl.multiple_of(group * 512 + 128 * h, 128), 128)] = value
    scale = lax.rsqrt(jnp.sum(squares, axis=-1, keepdims=True) / out.shape[1] + 1e-05)
    out[...] = (attended[...] * scale * gain[...]).astype(BF16)


def body(tokens, qkv_weight, log_decay, norm_gain):
    tok = tokens[0]
    n, d = tok.shape
    piece = ((17, 16, 128), BF16)
    pair = ((2, 17, 16, 128), BF16)
    slots = ((8, 17, 16, 128), BF16)
    factor = ((8, 16, 128), F32)

    back_moves = (down, up, two_back)
    *rates, entry, total, held = call(
        prepare,
        [((8, n), F32)] * 4 + [((n, 128), F32), ((16, 128), BF16), ((n, d), BF16)],
        log_decay[0],
        tok,
        far=1,
    )
    rates = [rates[0]] + [send(a, m) for a, m in zip(rates[1:], (up, down, two))]
    toks = [held, send(tok, up), send(tok, down)]
    toks.append(send(tok, two))
    weight = call(load, [(qkv_weight.shape, BF16)], qkv_weight, far=1)[0]

    half = ((n, 512), BF16)
    quarter = ((4, 64, 128), BF16)
    made = []
    for t, a in zip(toks, rates):
        after = (made[0][2],) if made else ()
        made.append(
            call(
                states,
                [half, half, quarter, quarter],
                t,
                weight,
                a,
                *after,
                flops=1 << 30,
                scratch=[((4, 128, 128), BF16)],
            )
        )
    own, partner = [made[0][2]], [send(made[0][3], other)]
    partner_total = send(total, other)
    for i, m in enumerate(back_moves):
        own.append(send(made[i + 1][2], m))
        partner.append(send(made[i + 1][3], crossed(m)))
    pieces = call(deal, [pair] * 4, *own, *partner, total, partner_total)
    pieces = exchange(pieces, (2, 1, 3), along_x)
    own_total = call(row_total, [piece], *pieces, scratch=[slots, factor])[0]

    parts = []
    for i in range(4):
        out = ((2, n, 512), BF16)
        parts += call(insides, [out], toks[i], weight, rates[i], *made[i][:2], flops=1 << 30)
    for i, m in enumerate(back_moves):
        parts[i + 1] = send(parts[i + 1], m)

    marked = call(mark, [((16, 128), BF16)], own_total)[0]
    far_total = send(own_total, far)
    near = [send(own_total, along_y(e)) for e in range(1, 4)]
    totals = [own_total, far_total]
    for e in range(1, 4):
        totals += [near[e - 1], send(far_total, along_y(e))]
    carried = call(carry, [((16, 16, 128), BF16)] * 8, marked, *pieces, *totals, scratch=[slots] * 2 + [factor] * 2)
    carried = exchange(carried, (4, 5, 2, 3, 6, 7, 1), along_row)
    out = call(
        final,
        [((n, d), BF16)],
        entry,
        norm_gain[None],
        *parts,
        *carried,
        scratch=[((16, 128, 128), BF16), ((n, d), F32)],
        space=jax.ShapeDtypeStruct,
    )[0]
    return out[None]


def solution(mesh):
    placed = (P("fsdp", "ctx", None), P(None, None, "fsdp"), P("fsdp", None, "ctx"), P())
    return jax.shard_map(body, mesh=mesh, in_specs=placed, out_specs=P("fsdp", "ctx", None), check_vma=False)
```

```python
import itertools

import jax
import jax.numpy as jnp
from jax import lax
from jax.experimental import pallas as pl
from jax.experimental.pallas import tpu as pltpu
from jax.sharding import PartitionSpec as P


F32 = jnp.float32
BF16 = jnp.bfloat16
BOTH = ("ctx", "fsdp")
VMEM = pl.BlockSpec(memory_space=pltpu.VMEM)


def pairs(move):
    flat = lambda y, z, x, c: (((y * 2 + z // 4) * 4 + x) * 2 + c) * 4 + z % 4
    every = itertools.product(range(4), range(8), range(4), range(2))
    return [(flat(*at), flat(*move(*at))) for at in every]


def send(a, move):
    return lax.ppermute(a, BOTH, pairs(move))


def up(y, z, x, c):
    return y, (z + 1) % 8, x, c


def down(y, z, x, c):
    return y, (z - 1) % 8, x, c


def up_two(y, z, x, c):
    return y, (z + 2) % 8, x, c


def down_two(y, z, x, c):
    return y, (z - 2) % 8, x, c


def other(y, z, x, c):
    return y, z, x, 1 - c


def along_x(d):
    return lambda y, z, x, c: (y, z, x ^ d, c)


def far(y, z, x, c):
    return y, (z + 4) % 8, x, c


def along_y(d):
    return lambda y, z, x, c: (y ^ d, z, x, c)


def exchange(parts, order, move):
    got = {d: send(parts[d], move(d)) for d in order}
    return [parts[0]] + [got[d] for d in range(1, len(parts))]


def silu(a):
    return a * jax.nn.sigmoid(a)


def dot(a, b, dims):
    return lax.dot_general(a, b, (dims, ((), ())), preferred_element_type=F32)


def call(kernel, outs, *args, flops=0, scratch=(), space=pltpu.VMEM, far=0):
    moved = sum(a.size * a.dtype.itemsize for a in args)
    near = len(args) - far
    held = [pltpu.with_memory_space_constraint(a, pltpu.VMEM) for a in args[:near]] + [
        pltpu.with_memory_space_constraint(a, pltpu.HBM) for a in args[near:]
    ]
    return pl.pallas_call(
        kernel,
        in_specs=[VMEM] * near + [pl.BlockSpec(memory_space=pltpu.HBM)] * far,
        out_specs=[VMEM] * len(outs),
        out_shape=[space(shape, dtype) for shape, dtype in outs],
        scratch_shapes=[pltpu.VMEM(shape, dtype) for shape, dtype in scratch] + [pltpu.SemaphoreType.DMA(())] * far,
        cost_estimate=pl.CostEstimate(flops=flops, bytes_accessed=moved, transcendentals=0),
        compiler_params=pltpu.CompilerParams(vmem_limit_bytes=24 << 20),
    )(*held)


def place():
    i = lax.axis_index("ctx")
    return lax.rem(i, 8), lax.div(i, 8)


def running(a, span=256):
    lane = lax.rem(lax.broadcasted_iota(jnp.int32, a.shape, 1), span)
    step = 1
    while step < span:
        a = a + jnp.where(lane >= step, pltpu.roll(a, step, axis=1), 0.0)
        step *= 2
    return a


SHIFTS = (0, 1, 3, 2)


def split(a):
    high = a.astype(BF16)
    rest = a - high.astype(F32)
    mid = rest.astype(BF16)
    return high, mid, (rest - mid.astype(F32)).astype(BF16)


def pack(column):
    lane = lax.broadcasted_iota(jnp.int32, (16, 128), 1)
    high, mid, low = (jnp.broadcast_to(a.astype(F32), (16, 128)) for a in split(column))
    return jnp.where(lane == 0, high, jnp.where(lane == 1, mid, jnp.where(lane == 2, low, 0.0))).astype(BF16)


def unpack(tile):
    a = tile.astype(F32)
    return a[:, 0:1] + a[:, 1:2] + a[:, 2:3]


def prepare(rates, tok, r0, r1, r2, r3, entry, total, second, held, sem):
    f = lax.axis_index("fsdp")
    copy = pltpu.make_async_copy(tok, held, sem)
    copy.start()
    cums = []
    for i, out in enumerate((r0, r1, r2, r3)):
        group = lax.rem(f + SHIFTS[i], 4)
        own = rates[0:4, :]
        for g in range(1, 4):
            own = jnp.where(group == g, rates[4 * g : 4 * g + 4, :], own)
        own = jnp.concatenate([own, jnp.zeros_like(own)], axis=0)
        out[...] = own
        cums.append(running(own)[:4])
    halves = running(own, 128)
    cum = jnp.concatenate(cums + [halves], axis=0)
    entry[...] = jnp.concatenate([jnp.exp(cum).T, jnp.zeros((256, 104), F32)], axis=1)
    total[...] = pack(cum[:16, 255:256])
    second[...] = jnp.broadcast_to(jnp.exp(halves[:, 255:256]), (8, 128))
    copy.wait()


def load(w, held, sem):
    copy = pltpu.make_async_copy(w, held, sem)
    copy.start()
    copy.wait()


def project(tok, w, c, j):
    return jnp.dot(tok[...], w[c, :, 256 * j : 256 * j + 256], preferred_element_type=F32)


def states_of(tok, w, cum, k_out, v_out, locals_out, span):
    ends = [cum[:, at + span - 1 : at + span] - cum[:, at : at + span] for at in range(0, 256, span)]
    tail = jnp.exp(jnp.concatenate(ends, axis=1)).T
    for j in range(2):
        pair = slice(256 * j, 256 * j + 256)
        k = silu(project(tok, w, 1, j)).astype(BF16)
        v = project(tok, w, 2, j).astype(BF16)
        k_out[:, pair] = k
        v_out[:, pair] = v
        for h in range(2):
            cols = slice(128 * h, 128 * h + 128)
            head = 2 * j + h
            scaled = (k[:, cols].astype(F32) * tail[:, head : head + 1]).astype(BF16)
            for i, local in enumerate(locals_out):
                rows = slice(span * i, span * i + span)
                local[head] = dot(scaled[rows], v[rows, cols], ((0,), (0,))).astype(BF16)


def states(tok, w, rates, *refs):
    k_out, v_out, local = refs[-3:]
    states_of(tok, w, running(rates[...]), k_out, v_out, [local], 256)


def two_rates(first, second):
    lane = lax.broadcasted_iota(jnp.int32, (8, 256), 1)
    return running(jnp.where(lane < 128, first[...], second[...]), 128)


def states_two(t0, t1, w, r0, r1, tok, k_out, v_out, local0, local1):
    tok[0:128, :] = t0[...]
    tok[128:256, :] = t1[...]
    states_of(tok, w, two_rates(r0, r1), k_out, v_out, [local0, local1], 128)


def insides_of(tok, w, cum, k_ref, v_ref, outs, span):
    col = cum.T
    t = lax.broadcasted_iota(jnp.int32, (span, span), 0)
    causal = t >= lax.broadcasted_iota(jnp.int32, (span, span), 1)
    for j in range(2):
        q = silu(project(tok, w, 0, j)).astype(BF16)
        for h in range(2):
            head = 2 * j + h
            cols = slice(128 * head, 128 * head + 128)
            for i, out in enumerate(outs):
                rows = slice(span * i, span * i + span)
                own = q[rows, 128 * h : 128 * h + 128]
                out[0, :, cols] = own
                scores = dot(own, k_ref[rows, cols], ((1,), (1,)))
                gaps = col[rows, head : head + 1] - cum[head : head + 1, rows]
                weights = (scores * jnp.exp(jnp.where(causal, gaps, -jnp.inf))).astype(BF16)
                value = jnp.dot(weights, v_ref[rows, cols], preferred_element_type=F32)
                out[1, :, cols] = value.astype(BF16)


def insides(tok, w, rates, k_ref, v_ref, out):
    insides_of(tok, w, running(rates[...]), k_ref, v_ref, [out], 256)


def insides_two(tok, w, r0, r1, k_ref, v_ref, out0, out1):
    insides_of(tok, w, two_rates(r0, r1), k_ref, v_ref, [out0, out1], 128)


def halve(s0, s1, s2, s3, s4, second, same, cross):
    core = lax.rem(place()[0], 2)
    for number, out in ((core, same), (1 - core, cross)):
        rows = pl.ds(pl.multiple_of(number * 64, 64), 64)
        for i, s in enumerate((s0, s1, s2)):
            out[4 * i : 4 * i + 4] = s[:, rows, :]
        for h in range(4):
            whole = s3[h, rows, :].astype(F32) * second[h : h + 1, :] + s4[h, rows, :].astype(F32)
            out[12 + h] = whole.astype(BF16)


def deal(own, partner, total, partner_total, *outs):
    p, _ = place()
    x, core = lax.div(p, 2), lax.rem(p, 2)
    for d in range(4):
        rows = pl.ds(pl.multiple_of(jnp.bitwise_xor(x, d) * 16, 16), 16)
        for block, half, log in ((core, own, total), (1 - core, partner, partner_total)):
            outs[d][block, 0:16] = half[:, rows, :]
            outs[d][block, 16] = log[...]


def arrange(natural, pieces):
    x = lax.div(place()[0], 2)
    for d in range(4):
        at = jnp.bitwise_xor(x, d) * 2
        for core in range(2):
            natural[at + core] = pieces[d][core]


def row_total(*refs):
    pieces, out, natural, decay = refs[:4], refs[4], refs[5], refs[6]
    arrange(natural, pieces)
    logs = jnp.zeros((16, 1), F32)
    for e in range(8):
        own = unpack(natural[e, 16])
        logs += own
        decay[e] = jnp.broadcast_to(jnp.exp(own), (16, 128))
    for h in range(16):
        run = natural[0, h].astype(F32)
        for e in range(1, 8):
            run = run * decay[e, h : h + 1, :] + natural[e, h].astype(F32)
        out[h] = run.astype(BF16)
    out[16] = pack(logs)


def mark(total, out):
    out[...] = total[16]


def carry(_, *refs):
    pieces, totals, outs, natural, rows, decay, row_decay = refs[:4], refs[4:12], refs[12:16], *refs[16:]
    p, r = place()
    x = lax.div(p, 2)
    arrange(natural, pieces)
    for d in range(8):
        rows[jnp.bitwise_xor(r, d)] = totals[d][...]
    for e in range(8):
        decay[e] = jnp.broadcast_to(jnp.exp(unpack(natural[e, 16])), (16, 128))
        row_decay[e] = jnp.broadcast_to(jnp.exp(jnp.where(e < r, unpack(rows[e, 16]), 0.0)), (16, 128))
    for h in range(16):
        run = jnp.zeros((16, 128), F32)
        for e in range(7):
            run = run * row_decay[e, h : h + 1, :] + jnp.where(e < r, rows[e, h].astype(F32), 0.0)
        for e in range(8):
            piece = natural[e, h].astype(F32)
            natural[e, h] = run.astype(BF16)
            run = run * decay[e, h : h + 1, :] + piece
    for d in range(4):
        for block in range(2):
            outs[d][block] = natural[jnp.bitwise_xor(x, d) * 2 + block, 0:16]


def gather(p0, p1, p2, p3, out):
    p, _ = place()
    x, core = lax.div(p, 2), lax.rem(p, 2)
    for d, piece in enumerate((p0, p1, p2, p3)):
        out[:, pl.ds(pl.multiple_of(jnp.bitwise_xor(x, d) * 16, 16), 16), :] = piece[1 - core]


def final(entry, gain, first_half, crossed, *refs):
    parts, pieces, out, memory, attended = refs[:5], refs[5:9], refs[9], refs[10], refs[11]
    p, _ = place()
    x, core = lax.div(p, 2), lax.rem(p, 2)
    f = lax.axis_index("fsdp")
    for d in range(4):
        at = core * 64 + jnp.bitwise_xor(x, d) * 16
        memory[:, pl.ds(pl.multiple_of(at, 16), 16), :] = pieces[d][core]
    memory[:, pl.ds(pl.multiple_of(64 - core * 64, 64), 64), :] = crossed[...]
    squares = [jnp.zeros((128, 128), F32)] * 2
    for i, shift in enumerate(SHIFTS):
        group = lax.rem(f + shift, 4)
        for h in range(4):
            cols = slice(128 * h, 128 * h + 128)
            head = 4 * i + h
            for half in range(2):
                rows = slice(128 * half, 128 * half + 128)
                part, at = (parts[i], rows) if i < 3 else (parts[3 + half], slice(0, 128))
                q = part[0, at, cols]
                value = part[1, at, cols].astype(F32)
                value += jnp.dot(q, memory[head], preferred_element_type=F32) * entry[rows, head : head + 1]
                if i == 3 and half == 1:
                    value += jnp.dot(q, first_half[h], preferred_element_type=F32) * entry[rows, 16 + h : 17 + h]
                squares[half] += value * value
                attended[rows, pl.ds(pl.multiple_of(group * 512 + 128 * h, 128), 128)] = value
    for half in range(2):
        rows = slice(128 * half, 128 * half + 128)
        scale = lax.rsqrt(jnp.sum(squares[half], axis=-1, keepdims=True) / out.shape[1] + 1e-05)
        out[rows, :] = (attended[rows, :] * scale * gain[...]).astype(BF16)


def body(tokens, qkv_weight, log_decay, norm_gain):
    tok = tokens[0]
    n, d = tok.shape
    slots = ((8, 17, 16, 128), BF16)
    factor = ((8, 16, 128), F32)
    state = ((4, 128, 128), BF16)
    half = ((n, 512), BF16)

    from_up = send(tok, up)
    from_down = send(tok, down)
    *rates, entry, total, second, held = call(
        prepare,
        [((8, n), F32)] * 4 + [((n, 128), F32), ((16, 128), BF16), ((8, 128), F32), ((n, d), BF16)],
        log_decay[0],
        tok,
        far=1,
    )
    rates = [rates[0]] + [
        send(a, m) for a, m in zip((*rates[1:], rates[3]), (up, down, up_two, down_two))
    ]
    partner_total = send(total, other)
    first = send(from_up[:128], up)
    last = send(from_down[128:], down)
    weight = call(load, [(qkv_weight.shape, BF16)], qkv_weight, far=1)[0]

    toks, made = [held, from_up, from_down], []
    for i in range(3):
        after = (made[0][2],) if made else ()
        made.append(call(states, [half, half, state], toks[i], weight, rates[i], *after, flops=1 << 30))
    two = call(
        states_two, [((n, d), BF16), half, half, state, state], first, last, weight, *rates[3:], flops=1 << 30
    )
    first_half, last_half = send(two[3], down_two), send(two[4], up_two)
    back_1 = send(made[1][2], down)
    back_2 = send(made[2][2], up)

    parts = []
    for i in range(3):
        parts += call(
            insides, [((2, n, 512), BF16)], toks[i], weight, rates[i], *made[i][:2], flops=1 << 30
        )
    parts += call(insides_two, [((2, 128, 512), BF16)] * 2, two[0], weight, *rates[3:], *two[1:3], flops=1 << 30)
    for i, m in enumerate((down, up, down_two, up_two)):
        parts[i + 1] = send(parts[i + 1], m)

    same, cross = call(
        halve, [((16, 64, 128), BF16)] * 2, made[0][2], back_1, back_2, first_half, last_half, second
    )
    partner = send(cross, other)
    pieces = call(deal, [((2, 17, 16, 128), BF16)] * 4, same, partner, total, partner_total)
    pieces = exchange(pieces, (2, 1, 3), along_x)
    own_total = call(row_total, [((17, 16, 128), BF16)], *pieces, scratch=[slots, factor])[0]

    marked = call(mark, [((16, 128), BF16)], own_total)[0]
    far_total = send(own_total, far)
    near = [send(own_total, along_y(e)) for e in range(1, 4)]
    totals = [own_total, far_total]
    for e in range(1, 4):
        totals += [near[e - 1], send(far_total, along_y(e))]
    carried = call(
        carry,
        [((2, 16, 16, 128), BF16)] * 4,
        marked,
        *pieces,
        *totals,
        scratch=[slots] * 2 + [factor] * 2,
    )
    carried = exchange(carried, (2, 1, 3), along_x)
    crossed = send(call(gather, [((16, 64, 128), BF16)], *carried)[0], other)
    out = call(
        final,
        [((n, d), BF16)],
        entry,
        norm_gain[None],
        first_half,
        crossed,
        *parts,
        *carried,
        scratch=[((16, 128, 128), BF16), ((n, d), F32)],
        space=jax.ShapeDtypeStruct,
    )[0]
    return out[None]


def solution(mesh):
    placed = (P("fsdp", "ctx", None), P(None, None, "fsdp"), P("fsdp", None, "ctx"), P())
    return jax.shard_map(body, mesh=mesh, in_specs=placed, out_specs=P("fsdp", "ctx", None), check_vma=False)
```

```python
import itertools

import jax
import jax.numpy as jnp
from jax import lax
from jax.experimental import pallas as pl
from jax.experimental.pallas import tpu as pltpu
from jax.sharding import PartitionSpec as P


F32 = jnp.float32
BF16 = jnp.bfloat16
BOTH = ("ctx", "fsdp")
VMEM = pl.BlockSpec(memory_space=pltpu.VMEM)


def pairs(move):
    flat = lambda y, z, x, c: (((y * 2 + z // 4) * 4 + x) * 2 + c) * 4 + z % 4
    every = itertools.product(range(4), range(8), range(4), range(2))
    return [(flat(*at), flat(*move(*at))) for at in every]


def send(a, move):
    return lax.ppermute(a, BOTH, pairs(move))


def up(y, z, x, c):
    return y, (z + 1) % 8, x, c


def down(y, z, x, c):
    return y, (z - 1) % 8, x, c


def up_two(y, z, x, c):
    return y, (z + 2) % 8, x, c


def down_two(y, z, x, c):
    return y, (z - 2) % 8, x, c


def other(y, z, x, c):
    return y, z, x, 1 - c


def along_x(d):
    return lambda y, z, x, c: (y, z, x ^ d, c)


def far(y, z, x, c):
    return y, (z + 4) % 8, x, c


def along_y(d):
    return lambda y, z, x, c: (y ^ d, z, x, c)


def exchange(parts, order, move):
    got = {d: send(parts[d], move(d)) for d in order}
    return [parts[0]] + [got[d] for d in range(1, len(parts))]


def silu(a):
    return a * jax.nn.sigmoid(a)


def dot(a, b, dims):
    return lax.dot_general(a, b, (dims, ((), ())), preferred_element_type=F32)


def call(kernel, outs, *args, flops=0, scratch=(), space=pltpu.VMEM, far=0):
    moved = sum(a.size * a.dtype.itemsize for a in args)
    near = len(args) - far
    held = [pltpu.with_memory_space_constraint(a, pltpu.VMEM) for a in args[:near]] + [
        pltpu.with_memory_space_constraint(a, pltpu.HBM) for a in args[near:]
    ]
    return pl.pallas_call(
        kernel,
        in_specs=[VMEM] * near + [pl.BlockSpec(memory_space=pltpu.HBM)] * far,
        out_specs=[VMEM] * len(outs),
        out_shape=[space(shape, dtype) for shape, dtype in outs],
        scratch_shapes=[pltpu.VMEM(shape, dtype) for shape, dtype in scratch] + [pltpu.SemaphoreType.DMA(())] * far,
        cost_estimate=pl.CostEstimate(flops=flops, bytes_accessed=moved, transcendentals=0),
        compiler_params=pltpu.CompilerParams(vmem_limit_bytes=24 << 20),
    )(*held)


def place():
    i = lax.axis_index("ctx")
    return lax.rem(i, 8), lax.div(i, 8)


def running(a, span=256):
    lane = lax.rem(lax.broadcasted_iota(jnp.int32, a.shape, 1), span)
    step = 1
    while step < span:
        a = a + jnp.where(lane >= step, pltpu.roll(a, step, axis=1), 0.0)
        step *= 2
    return a


SHIFTS = (0, 1, 3, 2)


def split(a):
    high = a.astype(BF16)
    rest = a - high.astype(F32)
    mid = rest.astype(BF16)
    return high, mid, (rest - mid.astype(F32)).astype(BF16)


def pack(column):
    lane = lax.broadcasted_iota(jnp.int32, (16, 128), 1)
    high, mid, low = (jnp.broadcast_to(a.astype(F32), (16, 128)) for a in split(column))
    return jnp.where(lane == 0, high, jnp.where(lane == 1, mid, jnp.where(lane == 2, low, 0.0))).astype(BF16)


def unpack(tile):
    a = tile.astype(F32)
    return a[:, 0:1] + a[:, 1:2] + a[:, 2:3]


def prepare(rates, tok, r0, r1, r2, r3, entry, total, second, held, sem):
    f = lax.axis_index("fsdp")
    copy = pltpu.make_async_copy(tok, held, sem)
    copy.start()
    cums = []
    for i, out in enumerate((r0, r1, r2, r3)):
        group = lax.rem(f + SHIFTS[i], 4)
        own = rates[0:4, :]
        for g in range(1, 4):
            own = jnp.where(group == g, rates[4 * g : 4 * g + 4, :], own)
        own = jnp.concatenate([own, jnp.zeros_like(own)], axis=0)
        out[...] = own
        cums.append(running(own)[:4])
    halves = running(own, 128)
    cum = jnp.concatenate(cums + [halves], axis=0)
    entry[...] = jnp.concatenate([jnp.exp(cum).T, jnp.zeros((256, 104), F32)], axis=1)
    total[...] = pack(cum[:16, 255:256])
    second[...] = jnp.broadcast_to(jnp.exp(halves[:, 255:256]), (8, 128))
    copy.wait()


def load(w, held, sem):
    copy = pltpu.make_async_copy(w, held, sem)
    copy.start()
    copy.wait()


def project(tok, w, c, j):
    return jnp.dot(tok[...], w[c, :, 256 * j : 256 * j + 256], preferred_element_type=F32)


def states_of(tok, w, cum, k_out, v_out, locals_out, span):
    ends = [cum[:, at + span - 1 : at + span] - cum[:, at : at + span] for at in range(0, 256, span)]
    tail = jnp.exp(jnp.concatenate(ends, axis=1)).T
    for j in range(2):
        pair = slice(256 * j, 256 * j + 256)
        k = silu(project(tok, w, 1, j)).astype(BF16)
        v = project(tok, w, 2, j).astype(BF16)
        k_out[:, pair] = k
        v_out[:, pair] = v
        for h in range(2):
            cols = slice(128 * h, 128 * h + 128)
            head = 2 * j + h
            scaled = (k[:, cols].astype(F32) * tail[:, head : head + 1]).astype(BF16)
            for i, local in enumerate(locals_out):
                rows = slice(span * i, span * i + span)
                local[head] = dot(scaled[rows], v[rows, cols], ((0,), (0,))).astype(BF16)


def states(tok, w, rates, *refs):
    k_out, v_out, local = refs[-3:]
    states_of(tok, w, running(rates[...]), k_out, v_out, [local], 256)


def states_joined(t0, t1, w, rates, *refs):
    tok, k_out, v_out, local = refs[-4:]
    tok[0:128, :] = t0[...]
    tok[128:256, :] = t1[...]
    states_of(tok, w, running(rates[...]), k_out, v_out, [local], 256)


def two_rates(first, second):
    lane = lax.broadcasted_iota(jnp.int32, (8, 256), 1)
    return running(jnp.where(lane < 128, first[...], second[...]), 128)


def states_two(t0, t1, w, r0, r1, tok, k_out, v_out, local0, local1):
    tok[0:128, :] = t0[...]
    tok[128:256, :] = t1[...]
    states_of(tok, w, two_rates(r0, r1), k_out, v_out, [local0, local1], 128)


def insides_of(tok, w, cum, k_ref, v_ref, outs, span):
    col = cum.T
    t = lax.broadcasted_iota(jnp.int32, (span, span), 0)
    causal = t >= lax.broadcasted_iota(jnp.int32, (span, span), 1)
    for j in range(2):
        q = silu(project(tok, w, 0, j)).astype(BF16)
        for h in range(2):
            head = 2 * j + h
            cols = slice(128 * head, 128 * head + 128)
            for i, out in enumerate(outs):
                rows = slice(span * i, span * i + span)
                own = q[rows, 128 * h : 128 * h + 128]
                out[0, :, cols] = own
                scores = dot(own, k_ref[rows, cols], ((1,), (1,)))
                gaps = col[rows, head : head + 1] - cum[head : head + 1, rows]
                weights = (scores * jnp.exp(jnp.where(causal, gaps, -jnp.inf))).astype(BF16)
                value = jnp.dot(weights, v_ref[rows, cols], preferred_element_type=F32)
                out[1, :, cols] = value.astype(BF16)


def insides(tok, w, rates, k_ref, v_ref, *refs):
    insides_of(tok, w, running(rates[...]), k_ref, v_ref, [refs[-1]], 256)


def insides_two(tok, w, r0, r1, k_ref, v_ref, out0, out1):
    insides_of(tok, w, two_rates(r0, r1), k_ref, v_ref, [out0, out1], 128)


def halve(s0, s1, s2, s3, s4, second, same, cross):
    core = lax.rem(place()[0], 2)
    for number, out in ((core, same), (1 - core, cross)):
        rows = pl.ds(pl.multiple_of(number * 64, 64), 64)
        for i, s in enumerate((s0, s1, s2)):
            out[4 * i : 4 * i + 4] = s[:, rows, :]
        for h in range(4):
            whole = s3[h, rows, :].astype(F32) * second[h : h + 1, :] + s4[h, rows, :].astype(F32)
            out[12 + h] = whole.astype(BF16)


def deal(own, partner, total, partner_total, *outs):
    p, _ = place()
    x, core = lax.div(p, 2), lax.rem(p, 2)
    for d in range(4):
        rows = pl.ds(pl.multiple_of(jnp.bitwise_xor(x, d) * 16, 16), 16)
        for block, half, log in ((core, own, total), (1 - core, partner, partner_total)):
            outs[d][block, 0:16] = half[:, rows, :]
            outs[d][block, 16] = log[...]


def arrange(natural, pieces):
    x = lax.div(place()[0], 2)
    for d in range(4):
        at = jnp.bitwise_xor(x, d) * 2
        for core in range(2):
            natural[at + core] = pieces[d][core]


def row_total(*refs):
    pieces, out, natural, decay = refs[:4], refs[4], refs[5], refs[6]
    arrange(natural, pieces)
    logs = jnp.zeros((16, 1), F32)
    for e in range(8):
        own = unpack(natural[e, 16])
        logs += own
        decay[e] = jnp.broadcast_to(jnp.exp(own), (16, 128))
    for h in range(16):
        run = natural[0, h].astype(F32)
        for e in range(1, 8):
            run = run * decay[e, h : h + 1, :] + natural[e, h].astype(F32)
        out[h] = run.astype(BF16)
    out[16] = pack(logs)


def mark(total, out):
    out[...] = total[16]


def carry(_, *refs):
    pieces, totals, outs, natural, rows, decay, row_decay = refs[:4], refs[4:12], refs[12:16], *refs[16:]
    p, r = place()
    x = lax.div(p, 2)
    arrange(natural, pieces)
    for d in range(8):
        rows[jnp.bitwise_xor(r, d)] = totals[d][...]
    for e in range(8):
        decay[e] = jnp.broadcast_to(jnp.exp(unpack(natural[e, 16])), (16, 128))
        row_decay[e] = jnp.broadcast_to(jnp.exp(jnp.where(e < r, unpack(rows[e, 16]), 0.0)), (16, 128))
    for h in range(16):
        run = jnp.zeros((16, 128), F32)
        for e in range(7):
            run = run * row_decay[e, h : h + 1, :] + jnp.where(e < r, rows[e, h].astype(F32), 0.0)
        for e in range(8):
            piece = natural[e, h].astype(F32)
            natural[e, h] = run.astype(BF16)
            run = run * decay[e, h : h + 1, :] + piece
    for d in range(4):
        for block in range(2):
            outs[d][block] = natural[jnp.bitwise_xor(x, d) * 2 + block, 0:16]


def gather(p0, p1, p2, p3, out):
    p, _ = place()
    x, core = lax.div(p, 2), lax.rem(p, 2)
    for d, piece in enumerate((p0, p1, p2, p3)):
        out[:, pl.ds(pl.multiple_of(jnp.bitwise_xor(x, d) * 16, 16), 16), :] = piece[1 - core]


def final(entry, gain, first_half, crossed, *refs):
    parts, pieces, out, memory, attended = refs[:5], refs[5:9], refs[9], refs[10], refs[11]
    p, _ = place()
    x, core = lax.div(p, 2), lax.rem(p, 2)
    f = lax.axis_index("fsdp")
    for d in range(4):
        at = core * 64 + jnp.bitwise_xor(x, d) * 16
        memory[:, pl.ds(pl.multiple_of(at, 16), 16), :] = pieces[d][core]
    memory[:, pl.ds(pl.multiple_of(64 - core * 64, 64), 64), :] = crossed[...]
    squares = [jnp.zeros((128, 128), F32)] * 2
    for i, shift in enumerate(SHIFTS):
        group = lax.rem(f + shift, 4)
        for h in range(4):
            cols = slice(128 * h, 128 * h + 128)
            head = 4 * i + h
            for half in range(2):
                rows = slice(128 * half, 128 * half + 128)
                part, at = (parts[i], rows) if i < 3 else (parts[3 + half], slice(0, 128))
                q = part[0, at, cols]
                value = part[1, at, cols].astype(F32)
                value += jnp.dot(q, memory[head], preferred_element_type=F32) * entry[rows, head : head + 1]
                if i == 3 and half == 1:
                    value += jnp.dot(q, first_half[h], preferred_element_type=F32) * entry[rows, 16 + h : 17 + h]
                squares[half] += value * value
                attended[rows, pl.ds(pl.multiple_of(group * 512 + 128 * h, 128), 128)] = value
    for half in range(2):
        rows = slice(128 * half, 128 * half + 128)
        scale = lax.rsqrt(jnp.sum(squares[half], axis=-1, keepdims=True) / out.shape[1] + 1e-05)
        out[rows, :] = (attended[rows, :] * scale * gain[...]).astype(BF16)


def body(tokens, qkv_weight, log_decay, norm_gain):
    tok = tokens[0]
    n, d = tok.shape
    slots = ((8, 17, 16, 128), BF16)
    factor = ((8, 16, 128), F32)
    state = ((4, 128, 128), BF16)
    half = ((n, 512), BF16)

    early, late = tok[:128], tok[128:]
    early_up, late_down = send(early, up), send(late, down)
    late_up, early_down = send(late, up), send(early, down)
    *rates, entry, total, second, held = call(
        prepare,
        [((8, n), F32)] * 4 + [((n, 128), F32), ((16, 128), BF16), ((8, 128), F32), ((n, d), BF16)],
        log_decay[0],
        tok,
        far=1,
    )
    rates = [rates[0]] + [
        send(a, m) for a, m in zip((*rates[1:], rates[3]), (up, down, up_two, down_two))
    ]
    partner_total = send(total, other)
    first = send(early_up, up)
    last = send(late_down, down)
    weight = call(load, [(qkv_weight.shape, BF16)], qkv_weight, far=1)[0]

    made = [[held, *call(states, [half, half, state], held, weight, rates[0], flops=1 << 30)]]
    for i, halves in ((1, (early_up, late_up)), (2, (early_down, late_down))):
        made.append(
            call(
                states_joined,
                [((n, d), BF16), half, half, state],
                *halves,
                weight,
                rates[i],
                made[0][3],
                flops=1 << 30,
            )
        )
    two = call(
        states_two, [((n, d), BF16), half, half, state, state], first, last, weight, *rates[3:], flops=1 << 30
    )
    first_half, last_half = send(two[3], down_two), send(two[4], up_two)
    back_1 = send(made[1][3], down)
    back_2 = send(made[2][3], up)

    last_parts = call(insides_two, [((2, 128, 512), BF16)] * 2, two[0], weight, *rates[3:], *two[1:3], flops=1 << 30)
    parts = []
    for i in range(3):
        after = (last_parts[0],) if i == 2 else ()
        parts += call(insides, [((2, n, 512), BF16)], made[i][0], weight, rates[i], *made[i][1:3], *after, flops=1 << 30)
    parts += last_parts
    for i, m in enumerate((down, up, down_two, up_two)):
        parts[i + 1] = send(parts[i + 1], m)

    same, cross = call(
        halve, [((16, 64, 128), BF16)] * 2, made[0][3], back_1, back_2, first_half, last_half, second
    )
    partner = send(cross, other)
    pieces = call(deal, [((2, 17, 16, 128), BF16)] * 4, same, partner, total, partner_total)
    pieces = exchange(pieces, (2, 1, 3), along_x)
    own_total = call(row_total, [((17, 16, 128), BF16)], *pieces, scratch=[slots, factor])[0]

    marked = call(mark, [((16, 128), BF16)], own_total)[0]
    far_total = send(own_total, far)
    near = [send(own_total, along_y(e)) for e in range(1, 4)]
    totals = [own_total, far_total]
    for e in range(1, 4):
        totals += [near[e - 1], send(far_total, along_y(e))]
    carried = call(
        carry,
        [((2, 16, 16, 128), BF16)] * 4,
        marked,
        *pieces,
        *totals,
        scratch=[slots] * 2 + [factor] * 2,
    )
    carried = exchange(carried, (2, 1, 3), along_x)
    crossed = send(call(gather, [((16, 64, 128), BF16)], *carried)[0], other)
    out = call(
        final,
        [((n, d), BF16)],
        entry,
        norm_gain[None],
        first_half,
        crossed,
        *parts,
        *carried,
        scratch=[((16, 128, 128), BF16), ((n, d), F32)],
        space=jax.ShapeDtypeStruct,
    )[0]
    return out[None]


def solution(mesh):
    placed = (P("fsdp", "ctx", None), P(None, None, "fsdp"), P("fsdp", None, "ctx"), P())
    return jax.shard_map(body, mesh=mesh, in_specs=placed, out_specs=P("fsdp", "ctx", None), check_vma=False)
```

```python
import itertools

import jax
import jax.numpy as jnp
from jax import lax
from jax.experimental import pallas as pl
from jax.experimental.pallas import tpu as pltpu
from jax.sharding import PartitionSpec as P


F32 = jnp.float32
BF16 = jnp.bfloat16
BOTH = ("ctx", "fsdp")
VMEM = pl.BlockSpec(memory_space=pltpu.VMEM)


def pairs(move):
    flat = lambda y, z, x, c: (((y * 2 + z // 4) * 4 + x) * 2 + c) * 4 + z % 4
    every = itertools.product(range(4), range(8), range(4), range(2))
    return [(flat(*at), flat(*move(*at))) for at in every]


def send(a, move):
    return lax.ppermute(a, BOTH, pairs(move))


def up(y, z, x, c):
    return y, (z + 1) % 8, x, c


def down(y, z, x, c):
    return y, (z - 1) % 8, x, c


def up_two(y, z, x, c):
    return y, (z + 2) % 8, x, c


def down_two(y, z, x, c):
    return y, (z - 2) % 8, x, c


def other(y, z, x, c):
    return y, z, x, 1 - c


def along_x(d):
    return lambda y, z, x, c: (y, z, x ^ d, c)


def far(y, z, x, c):
    return y, (z + 4) % 8, x, c


def along_y(d):
    return lambda y, z, x, c: (y ^ d, z, x, c)


def exchange(parts, order, move):
    got = {d: send(parts[d], move(d)) for d in order}
    return [parts[0]] + [got[d] for d in range(1, len(parts))]


def silu(a):
    return a * jax.nn.sigmoid(a)


def dot(a, b, dims):
    return lax.dot_general(a, b, (dims, ((), ())), preferred_element_type=F32)


def call(kernel, outs, *args, flops=0, scratch=(), far=0):
    moved = sum(a.size * a.dtype.itemsize for a in args)
    near = len(args) - far
    held = [pltpu.with_memory_space_constraint(a, pltpu.VMEM) for a in args[:near]] + [
        pltpu.with_memory_space_constraint(a, pltpu.HBM) for a in args[near:]
    ]
    return pl.pallas_call(
        kernel,
        in_specs=[VMEM] * near + [pl.BlockSpec(memory_space=pltpu.HBM)] * far,
        out_specs=[VMEM] * len(outs),
        out_shape=[pltpu.VMEM(shape, dtype) for shape, dtype in outs],
        scratch_shapes=[pltpu.VMEM(shape, dtype) for shape, dtype in scratch] + [pltpu.SemaphoreType.DMA(())] * far,
        cost_estimate=pl.CostEstimate(flops=flops, bytes_accessed=moved, transcendentals=0),
        compiler_params=pltpu.CompilerParams(vmem_limit_bytes=24 << 20),
    )(*held)


def place():
    i = lax.axis_index("ctx")
    return lax.rem(i, 8), lax.div(i, 8)


def running(a, span=256):
    lane = lax.rem(lax.broadcasted_iota(jnp.int32, a.shape, 1), span)
    step = 1
    while step < span:
        a = a + jnp.where(lane >= step, pltpu.roll(a, step, axis=1), 0.0)
        step *= 2
    return a


SHIFTS = (0, 1, 3, 2)


def split(a):
    high = a.astype(BF16)
    rest = a - high.astype(F32)
    mid = rest.astype(BF16)
    return high, mid, (rest - mid.astype(F32)).astype(BF16)


def pack(column):
    lane = lax.broadcasted_iota(jnp.int32, (16, 128), 1)
    high, mid, low = (jnp.broadcast_to(a.astype(F32), (16, 128)) for a in split(column))
    return jnp.where(lane == 0, high, jnp.where(lane == 1, mid, jnp.where(lane == 2, low, 0.0))).astype(BF16)


def unpack(tile):
    a = tile.astype(F32)
    return a[:, 0:1] + a[:, 1:2] + a[:, 2:3]


def prepare(rates, tok, r0, r1, r2, r3, entry, total, second, held, sem):
    f = lax.axis_index("fsdp")
    copy = pltpu.make_async_copy(tok, held, sem)
    copy.start()
    cums = []
    for i, out in enumerate((r0, r1, r2, r3)):
        group = lax.rem(f + SHIFTS[i], 4)
        own = rates[0:4, :]
        for g in range(1, 4):
            own = jnp.where(group == g, rates[4 * g : 4 * g + 4, :], own)
        own = jnp.concatenate([own, jnp.zeros_like(own)], axis=0)
        out[...] = own
        cums.append(running(own)[:4])
    halves = running(own, 128)
    cum = jnp.concatenate(cums + [halves], axis=0)
    entry[...] = jnp.concatenate([jnp.exp(cum).T, jnp.zeros((256, 104), F32)], axis=1)
    total[...] = pack(cum[:16, 255:256])
    second[...] = jnp.broadcast_to(jnp.exp(halves[:, 255:256]), (8, 128))
    copy.wait()


def load(w, held, sem):
    copy = pltpu.make_async_copy(w, held, sem)
    copy.start()
    copy.wait()


def project(tok, w, c, j):
    return jnp.dot(tok[...], w[c, :, 256 * j : 256 * j + 256], preferred_element_type=F32)


def states_of(tok, w, cum, k_out, v_out, locals_out, span):
    ends = [cum[:, at + span - 1 : at + span] - cum[:, at : at + span] for at in range(0, 256, span)]
    tail = jnp.exp(jnp.concatenate(ends, axis=1)).T
    for j in range(2):
        pair = slice(256 * j, 256 * j + 256)
        k = silu(project(tok, w, 1, j)).astype(BF16)
        v = project(tok, w, 2, j).astype(BF16)
        k_out[:, pair] = k
        v_out[:, pair] = v
        for h in range(2):
            cols = slice(128 * h, 128 * h + 128)
            head = 2 * j + h
            scaled = (k[:, cols].astype(F32) * tail[:, head : head + 1]).astype(BF16)
            for i, local in enumerate(locals_out):
                rows = slice(span * i, span * i + span)
                local[head] = dot(scaled[rows], v[rows, cols], ((0,), (0,))).astype(BF16)


def states(tok, w, rates, *refs):
    k_out, v_out, local = refs[-3:]
    states_of(tok, w, running(rates[...]), k_out, v_out, [local], 256)


def states_joined(t0, t1, w, rates, *refs):
    tok, k_out, v_out, local = refs[-4:]
    tok[0:128, :] = t0[...]
    tok[128:256, :] = t1[...]
    states_of(tok, w, running(rates[...]), k_out, v_out, [local], 256)


def two_rates(first, second):
    lane = lax.broadcasted_iota(jnp.int32, (8, 256), 1)
    return running(jnp.where(lane < 128, first[...], second[...]), 128)


def states_two(t0, t1, w, r0, r1, tok, k_out, v_out, local0, local1):
    tok[0:128, :] = t0[...]
    tok[128:256, :] = t1[...]
    states_of(tok, w, two_rates(r0, r1), k_out, v_out, [local0, local1], 128)


def insides_of(tok, w, cum, k_ref, v_ref, outs, span):
    col = cum.T
    t = lax.broadcasted_iota(jnp.int32, (span, span), 0)
    causal = t >= lax.broadcasted_iota(jnp.int32, (span, span), 1)
    for j in range(2):
        q = silu(project(tok, w, 0, j)).astype(BF16)
        for h in range(2):
            head = 2 * j + h
            cols = slice(128 * head, 128 * head + 128)
            for i, out in enumerate(outs):
                rows = slice(span * i, span * i + span)
                own = q[rows, 128 * h : 128 * h + 128]
                out[0, :, cols] = own
                scores = dot(own, k_ref[rows, cols], ((1,), (1,)))
                gaps = col[rows, head : head + 1] - cum[head : head + 1, rows]
                weights = (scores * jnp.exp(jnp.where(causal, gaps, -jnp.inf))).astype(BF16)
                value = jnp.dot(weights, v_ref[rows, cols], preferred_element_type=F32)
                out[1, :, cols] = value.astype(BF16)


def insides(tok, w, rates, k_ref, v_ref, *refs):
    insides_of(tok, w, running(rates[...]), k_ref, v_ref, [refs[-1]], 256)


def insides_first(tok, w, rates, k_ref, v_ref, s1, s2, out, t1, t2):
    t1[...] = s1[...]
    t2[...] = s2[...]
    insides_of(tok, w, running(rates[...]), k_ref, v_ref, [out], 256)


def insides_two(tok, w, r0, r1, k_ref, v_ref, out0, out1):
    insides_of(tok, w, two_rates(r0, r1), k_ref, v_ref, [out0, out1], 128)


def halve(s0, s1, s2, s3, s4, second, same, cross):
    core = lax.rem(place()[0], 2)
    for number, out in ((core, same), (1 - core, cross)):
        rows = pl.ds(pl.multiple_of(number * 64, 64), 64)
        for i, s in enumerate((s0, s1, s2)):
            out[4 * i : 4 * i + 4] = s[:, rows, :]
        for h in range(4):
            whole = s3[h, rows, :].astype(F32) * second[h : h + 1, :] + s4[h, rows, :].astype(F32)
            out[12 + h] = whole.astype(BF16)


def deal(own, partner, total, partner_total, *outs):
    p, _ = place()
    x, core = lax.div(p, 2), lax.rem(p, 2)
    for d in range(4):
        rows = pl.ds(pl.multiple_of(jnp.bitwise_xor(x, d) * 16, 16), 16)
        for block, half, log in ((core, own, total), (1 - core, partner, partner_total)):
            outs[d][block, 0:16] = half[:, rows, :]
            outs[d][block, 16] = log[...]


def arrange(natural, pieces):
    x = lax.div(place()[0], 2)
    for d in range(4):
        at = jnp.bitwise_xor(x, d) * 2
        for core in range(2):
            natural[at + core] = pieces[d][core]


def row_total(*refs):
    pieces, out, natural, decay = refs[:4], refs[4], refs[5], refs[6]
    arrange(natural, pieces)
    logs = jnp.zeros((16, 1), F32)
    for e in range(8):
        own = unpack(natural[e, 16])
        logs += own
        decay[e] = jnp.broadcast_to(jnp.exp(own), (16, 128))
    for h in range(16):
        run = natural[0, h].astype(F32)
        for e in range(1, 8):
            run = run * decay[e, h : h + 1, :] + natural[e, h].astype(F32)
        out[h] = run.astype(BF16)
    out[16] = pack(logs)


def mark(total, out):
    out[...] = total[16]


def carry(_, *refs):
    pieces, totals, outs, natural, rows, decay, row_decay = refs[:4], refs[4:12], refs[12:16], *refs[16:]
    p, r = place()
    x = lax.div(p, 2)
    arrange(natural, pieces)
    for d in range(8):
        rows[jnp.bitwise_xor(r, d)] = totals[d][...]
    for e in range(8):
        decay[e] = jnp.broadcast_to(jnp.exp(unpack(natural[e, 16])), (16, 128))
        row_decay[e] = jnp.broadcast_to(jnp.exp(jnp.where(e < r, unpack(rows[e, 16]), 0.0)), (16, 128))
    for h in range(16):
        run = jnp.zeros((16, 128), F32)
        for e in range(7):
            run = run * row_decay[e, h : h + 1, :] + jnp.where(e < r, rows[e, h].astype(F32), 0.0)
        for e in range(8):
            piece = natural[e, h].astype(F32)
            natural[e, h] = run.astype(BF16)
            run = run * decay[e, h : h + 1, :] + piece
    for d in range(4):
        for block in range(2):
            outs[d][block] = natural[jnp.bitwise_xor(x, d) * 2 + block, 0:16]


def gather(p0, p1, p2, p3, out):
    p, _ = place()
    x, core = lax.div(p, 2), lax.rem(p, 2)
    for d, piece in enumerate((p0, p1, p2, p3)):
        out[:, pl.ds(pl.multiple_of(jnp.bitwise_xor(x, d) * 16, 16), 16), :] = piece[1 - core]


def final(entry, gain, first_half, crossed, *refs):
    parts, pieces, out, memory, attended, normed, sems = refs[:5], refs[5:9], *refs[9:]
    p, _ = place()
    x, core = lax.div(p, 2), lax.rem(p, 2)
    f = lax.axis_index("fsdp")
    for d in range(4):
        at = core * 64 + jnp.bitwise_xor(x, d) * 16
        memory[:, pl.ds(pl.multiple_of(at, 16), 16), :] = pieces[d][core]
    memory[:, pl.ds(pl.multiple_of(64 - core * 64, 64), 64), :] = crossed[...]
    copies = []
    for half in range(2):
        rows = slice(128 * half, 128 * half + 128)
        squares = jnp.zeros((128, 128), F32)
        for i, shift in enumerate(SHIFTS):
            group = lax.rem(f + shift, 4)
            part, at = (parts[i], rows) if i < 3 else (parts[3 + half], slice(0, 128))
            for h in range(4):
                cols = slice(128 * h, 128 * h + 128)
                head = 4 * i + h
                q = part[0, at, cols]
                value = part[1, at, cols].astype(F32)
                value += jnp.dot(q, memory[head], preferred_element_type=F32) * entry[rows, head : head + 1]
                if i == 3 and half == 1:
                    value += jnp.dot(q, first_half[h], preferred_element_type=F32) * entry[rows, 16 + h : 17 + h]
                squares += value * value
                attended[:, pl.ds(pl.multiple_of(group * 512 + 128 * h, 128), 128)] = value
        scale = lax.rsqrt(jnp.sum(squares, axis=-1, keepdims=True) / out.shape[1] + 1e-05)
        normed[rows, :] = (attended[...] * scale * gain[...]).astype(BF16)
        copies.append(pltpu.make_async_copy(normed.at[rows, :], out.at[rows, :], sems.at[half]))
        copies[-1].start()
    for copy in copies:
        copy.wait()


def body(tokens, qkv_weight, log_decay, norm_gain):
    tok = tokens[0]
    n, d = tok.shape
    slots = ((8, 17, 16, 128), BF16)
    factor = ((8, 16, 128), F32)
    state = ((4, 128, 128), BF16)
    half = ((n, 512), BF16)

    early, late = tok[:128], tok[128:]
    early_up, late_down = send(early, up), send(late, down)
    late_up, early_down = send(late, up), send(early, down)
    *rates, entry, total, second, held = call(
        prepare,
        [((8, n), F32)] * 4 + [((n, 128), F32), ((16, 128), BF16), ((8, 128), F32), ((n, d), BF16)],
        log_decay[0],
        tok,
        far=1,
    )
    rates = [rates[0]] + [
        send(a, m) for a, m in zip((*rates[1:], rates[3]), (up, down, up_two, down_two))
    ]
    partner_total = send(total, other)
    first = send(early_up, up)
    last = send(late_down, down)
    weight = call(load, [(qkv_weight.shape, BF16)], qkv_weight, far=1)[0]

    made = [[held, *call(states, [half, half, state], held, weight, rates[0], flops=1 << 30)]]
    for i, halves in ((1, (early_up, late_up)), (2, (early_down, late_down))):
        made.append(
            call(
                states_joined,
                [((n, d), BF16), half, half, state],
                *halves,
                weight,
                rates[i],
                made[0][3],
                flops=1 << 30,
            )
        )
    middle, state_1, state_2 = call(
        insides_first,
        [((2, n, 512), BF16), state, state],
        made[1][0],
        weight,
        rates[1],
        *made[1][1:],
        made[2][3],
        flops=1 << 30,
    )
    two = call(
        states_two, [((n, d), BF16), half, half, state, state], first, last, weight, *rates[3:], flops=1 << 30
    )
    first_half, last_half = send(two[3], down_two), send(two[4], up_two)
    back_1 = send(state_1, down)
    back_2 = send(state_2, up)

    last_parts = call(insides_two, [((2, 128, 512), BF16)] * 2, two[0], weight, *rates[3:], *two[1:3], flops=1 << 30)
    parts = []
    for i in (0, 2):
        after = (last_parts[0],) if i == 2 else ()
        parts += call(insides, [((2, n, 512), BF16)], made[i][0], weight, rates[i], *made[i][1:3], *after, flops=1 << 30)
    parts = [parts[0], middle, parts[1], *last_parts]
    for i, m in enumerate((down, up, down_two, up_two)):
        parts[i + 1] = send(parts[i + 1], m)

    same, cross = call(
        halve, [((16, 64, 128), BF16)] * 2, made[0][3], back_1, back_2, first_half, last_half, second
    )
    partner = send(cross, other)
    pieces = call(deal, [((2, 17, 16, 128), BF16)] * 4, same, partner, total, partner_total)
    pieces = exchange(pieces, (2, 1, 3), along_x)
    own_total = call(row_total, [((17, 16, 128), BF16)], *pieces, scratch=[slots, factor])[0]

    marked = call(mark, [((16, 128), BF16)], own_total)[0]
    far_total = send(own_total, far)
    near = [send(own_total, along_y(e)) for e in range(1, 4)]
    totals = [own_total, far_total]
    for e in range(1, 4):
        totals += [near[e - 1], send(far_total, along_y(e))]
    carried = call(
        carry,
        [((2, 16, 16, 128), BF16)] * 4,
        marked,
        *pieces,
        *totals,
        scratch=[slots] * 2 + [factor] * 2,
    )
    carried = exchange(carried, (2, 1, 3), along_x)
    crossed = send(call(gather, [((16, 64, 128), BF16)], *carried)[0], other)
    args = (entry, norm_gain[None], first_half, crossed, *parts, *carried)
    out = pl.pallas_call(
        final,
        in_specs=[VMEM] * len(args),
        out_specs=pl.BlockSpec(memory_space=pltpu.HBM),
        out_shape=jax.ShapeDtypeStruct((n, d), BF16),
        scratch_shapes=[
            pltpu.VMEM((16, 128, 128), BF16),
            pltpu.VMEM((128, d), F32),
            pltpu.VMEM((n, d), BF16),
            pltpu.SemaphoreType.DMA((2,)),
        ],
        compiler_params=pltpu.CompilerParams(vmem_limit_bytes=24 << 20),
        name="final",
    )(*(pltpu.with_memory_space_constraint(a, pltpu.VMEM) for a in args))
    return out[None]


def solution(mesh):
    placed = (P("fsdp", "ctx", None), P(None, None, "fsdp"), P("fsdp", None, "ctx"), P())
    return jax.shard_map(body, mesh=mesh, in_specs=placed, out_specs=P("fsdp", "ctx", None), check_vma=False)
```
